256 devices in a mesh: pole: 4 (over y), row: 8 (over z_lo, x), col: 8 (over z_hi, core).
Axes of the slice: x: 4, y: 4, z: 8 (z_hi: 4, z_lo: 2; z = z_hi * 2 + z_lo), core: 2. Of those that a mesh axis runs over, the one named last changes fastest.
Arguments:
- found_inverse: bfloat16 [4, 2, 8192, 8, 8, 128], P('pole', None, 'row', None, 'col'), may hold values from -0.125 to 0.125
- l_panel: bfloat16 [4, 2, 8192, 512], P('pole', None, ('row', 'col')), may hold values from -1.5 to 1.5
- block_pattern: int32 [64, 4], P(('row', 'col')), may hold values 0 or 1
- sup_widths: int32 [4], replicated, may hold values from 1 to 128, 320 in all
- diag_inverse: bfloat16 [4, 2, 512, 128], P('pole'), may hold values from -6 to 6
- pole_weights: float32 [4, 2], P('pole'), may hold values from -4 to 4
Outputs:
- density: float32 [512, 8192], P('col', 'row')
- diagonal: float32 [512, 128], replicated
The draws below stay inside these ranges and needn't reach their ends.
Inputs may be any that keep to these rules, and one draw needn't show every extreme that they name: `sup_widths`: one supernode has exactly 128 columns.
All inputs are finite; a program needn't handle non-finite values. No bound on the sum of `block_pattern` on one device may be relied on, other than what follows from the above.
Results may differ from the reference program's by a relative error of at most 0.0003.
Values may be sent and summed in bfloat16 or wider, within the bound.
A program may use at most 128 MiB of HBM per device.

```python
import math
import jax
import jax.numpy as jnp
import numpy as np
from jax import lax

S = 128
NSUP = 4
POLES = 4
NB = 64
N = 8192
W = 512
N_ROW = 8
N_COL = 8


def with_ends(drawn, own_key, least, high):
    shape = drawn.shape
    index_at = [jax.random.randint(jax.random.fold_in(own_key, axis), (), 0, shape[axis]) for axis in range(len(shape))]
    drawn = drawn.at[tuple(index_at)].set(least)
    longest = shape.index(max(shape))
    index_at[longest] = (index_at[longest] + 1) % shape[longest]
    return drawn.at[tuple(index_at)].set(high)


def block_scale(stream_key, shape, shards, smallest, largest):
    gain = 1.0
    for position, parts in shards:
        steps = jax.random.uniform(jax.random.fold_in(jax.random.fold_in(stream_key, 6), position), (parts,), jnp.float32, smallest / len(shards), largest / len(shards))
        gain = gain * jnp.repeat(jnp.exp(steps), shape[position] // parts).reshape((-1,) + (1,) * (len(shape) - 1 - position))
    return gain


def profile(count, total, most, skew):
    portions = [(1 << 20) // math.isqrt(standing ** skew) + 1 for standing in range(2, count + 1)]
    surplus, given = total - most - (count - 1), [1] * (count - 1)
    while surplus > 0:
        movable = [i for i in range(count - 1) if given[i] < most]
        mass, budget = sum([portions[i] for i in movable]), surplus
        for i in movable:
            extra = min(most - given[i], max(1, budget * portions[i] // mass), surplus)
            given[i] = given[i] + extra
            surplus = surplus - extra
    return np.array([most] + given)


def uneven_parts(key, count, total, most, skew):
    if count == 2:
        one = jax.random.randint(key, (), max(1, total - most), min(most, total - 1) + 1)
        return jnp.stack([one, total - one])
    sizes = jnp.asarray(profile(count, total, most, skew), jnp.int32)
    couples = (count - 1) // 2
    donor, sink = sizes[1:1 + 2 * couples:2], sizes[2:2 + 2 * couples:2]
    room = jnp.minimum(donor - 1, most - sink)
    passed = jax.random.randint(jax.random.fold_in(key, 1), (couples,), 0, 1 << 20) % (room + 1)
    sizes = sizes.at[1:1 + 2 * couples:2].set(donor - passed).at[2:2 + 2 * couples:2].set(sink + passed)
    return sizes[jax.random.permutation(jax.random.fold_in(key, 2), count)]


def normal_values(rng, dims, scale, reach, cuts=(), held_as=jnp.bfloat16):
    gain = block_scale(rng, dims, cuts, -0.22, 0.18) if cuts else 1.0
    entries = jax.random.normal(rng, dims, jnp.float32) * scale * gain
    return jnp.minimum(jnp.maximum(entries, -reach), reach).astype(held_as)


def setup_inputs(seed: int = 0) -> dict:
    seeds = jax.random.split(jax.random.key(seed), 7)
    return {
        "found_inverse": normal_values(seeds[0], (POLES, 2, N, N_ROW, N_COL, S), (N // 4) ** -0.5, 0.125, ((0, 4), (2, 8), (4, 8))),
        "l_panel": normal_values(seeds[1], (POLES, 2, N, W), 0.25, 1.5, ((0, 4), (2, 64))),
        "block_pattern": with_ends((jax.random.randint(seeds[2], (NB, NSUP), 0, 2) < 1).astype(jnp.int32), jax.random.fold_in(seeds[2], 1), 0, 1),
        "sup_widths": uneven_parts(seeds[3], NSUP, S + (NSUP - 1) * (S // 2), S, 0).astype(jnp.int32),
        "diag_inverse": normal_values(seeds[4], (POLES, 2, W, S), 1.0, 6.0, ((0, 4),)),
        "pole_weights": normal_values(seeds[5], (POLES, 2), 1.0, 4.0, ((0, 4),), jnp.float32),
    }


def product(left, right):
    return jnp.dot(left, right, preferred_element_type=jnp.float32)


def pair_product(left, right):
    return jnp.einsum('ika,ikb->kab', left, right, precision=lax.Precision.HIGHEST)


def reference(found_inverse, l_panel, block_pattern, sup_widths, diag_inverse, pole_weights):
    slot_width = diag_inverse.shape[-1]
    supernodes = sup_widths.shape[0]
    total_cols = supernodes * slot_width
    order = l_panel.shape[2]
    columns = jnp.arange(total_cols, dtype=jnp.int32)
    column_ok = (columns % slot_width) < jnp.repeat(sup_widths, slot_width)
    row_valid = jnp.repeat(jnp.repeat(block_pattern, slot_width, axis=0), slot_width, axis=1) == 1
    keep_mask = row_valid & column_ok[None, :]
    density = jnp.zeros((order, total_cols), jnp.float32)
    diagonal = jnp.zeros((total_cols, slot_width), jnp.float32)
    for pole in range(POLES):
        masked = jnp.where(keep_mask[None], l_panel[pole], jnp.zeros((), jnp.bfloat16))
        inverse = found_inverse[pole].reshape(2, order, order)
        block_real = -(product(inverse[0], masked[0]) - product(inverse[1], masked[1]))
        block_imag = -(product(inverse[0], masked[1]) + product(inverse[1], masked[0]))
        w_real = pole_weights[pole, 0]
        w_imag = pole_weights[pole, 1]
        density = density + (w_real * block_real - w_imag * block_imag)
        lifted = masked.astype(jnp.float32).reshape(2, order, supernodes, slot_width)
        upper_real = block_real.reshape(order, supernodes, slot_width)
        upper_imag = block_imag.reshape(order, supernodes, slot_width)
        t_real = pair_product(lifted[0], upper_real) - pair_product(lifted[1], upper_imag)
        t_imag = pair_product(lifted[0], upper_imag) + pair_product(lifted[1], upper_real)
        d_real = diag_inverse[pole, 0].astype(jnp.float32).reshape(supernodes, slot_width, slot_width)
        d_imag = diag_inverse[pole, 1].astype(jnp.float32).reshape(supernodes, slot_width, slot_width)
        update = w_real * (d_real - t_real) - w_imag * (d_imag - t_imag)
        diagonal = diagonal + update.reshape(total_cols, slot_width)
    return density.T, diagonal
```

```python
import jax
import jax.numpy as jnp
from jax import lax
from jax.sharding import PartitionSpec as P


def contract(left, right):
    return jnp.einsum("jk,ij->ki", left, right, preferred_element_type=jnp.float32)


def pair_product(left, right):
    return jnp.einsum("ika,kbi->kab", left, right, precision=lax.Precision.HIGHEST)


def per_device(found_inverse, l_panel, block_pattern, sup_widths, diag_inverse, pole_weights):
    slot_width = diag_inverse.shape[-1]
    total_cols = l_panel.shape[-1]
    supernodes = total_cols // slot_width
    row_count = lax.axis_size("row")
    row_index = lax.axis_index("row")
    col_index = lax.axis_index("col")
    columns = jnp.arange(total_cols, dtype=jnp.int32)
    column_ok = columns % slot_width < jnp.repeat(sup_widths, slot_width)
    block_ok = jnp.repeat(block_pattern[0], slot_width) == 1
    masked = jnp.where(
        (column_ok & block_ok)[None, None, :], l_panel[0], jnp.zeros((), jnp.bfloat16)
    )
    column_rows = lax.all_gather(masked, "row", axis=1, tiled=True)
    own_rows = lax.all_gather(masked, "col", axis=1, tiled=True)
    local_rows = found_inverse.shape[2]
    inverse = found_inverse[0].reshape(2, local_rows, row_count * slot_width)
    part_real = contract(column_rows[1], inverse[1]) - contract(column_rows[0], inverse[0])
    part_imag = -(contract(column_rows[1], inverse[0]) + contract(column_rows[0], inverse[1]))
    w_real = pole_weights[0, 0]
    w_imag = pole_weights[0, 1]
    weighted = w_real * part_real - w_imag * part_imag
    part = lax.psum_scatter(weighted, "col", scatter_dimension=0, tiled=True)
    density = lax.psum(part, "pole")
    lifted = own_rows.astype(jnp.float32).reshape(2, local_rows, supernodes, slot_width)
    upper_real = part_real.reshape(supernodes, slot_width, local_rows)
    upper_imag = part_imag.reshape(supernodes, slot_width, local_rows)
    t_real = pair_product(lifted[0], upper_real) - pair_product(lifted[1], upper_imag)
    t_imag = pair_product(lifted[0], upper_imag) + pair_product(lifted[1], upper_real)
    lead_flag = ((row_index == 0) & (col_index == 0)).astype(jnp.float32)
    d_real = diag_inverse[0, 0].astype(jnp.float32).reshape(supernodes, slot_width, slot_width)
    d_imag = diag_inverse[0, 1].astype(jnp.float32).reshape(supernodes, slot_width, slot_width)
    local_term = lead_flag * (w_real * d_real - w_imag * d_imag) - (
        w_real * t_real - w_imag * t_imag
    )
    diagonal = lax.psum(local_term.reshape(total_cols, slot_width), ("pole", "row", "col"))
    return (density, diagonal)


def solution(mesh):
    in_specs = (
        P("pole", None, "row", None, "col", None),
        P("pole", None, ("row", "col"), None),
        P(("row", "col"), None),
        P(),
        P("pole", None, None, None),
        P("pole", None),
    )
    out_specs = (P("col", "row"), P())
    return jax.shard_map(
        per_device, mesh=mesh, in_specs=in_specs, out_specs=out_specs, check_vma=False
    )
```

```python
import functools

import jax
import jax.numpy as jnp
from jax import lax
from jax.experimental import pallas as pl
from jax.experimental.pallas import tpu as pltpu
from jax.sharding import PartitionSpec as P

MESH = pl.DeviceIdType.MESH
PACKED = 320
F32, BF16 = jnp.float32, jnp.bfloat16


def nt(left, right):
    return lax.dot_general(left, right, (((1,), (1,)), ((), ())), preferred_element_type=F32)


def nn(left, right):
    return lax.dot_general(left, right, (((1,), (0,)), ((), ())), preferred_element_type=F32)


def split(value):
    high = value.astype(BF16)
    return high, (value - high.astype(F32)).astype(BF16)


NAMES = (
    ["c_z", "c_xp", "c_xm", "c_zxp", "c_zxm", "c_x2", "c_zx2"]
    + ["m_p", "m_m", "m_2", "m_k0", "m_k1", "m_k2", "m_k3"]
    + ["x_core"]
    + [f"x_y{i}" for i in range(3)]
    + [f"x_z{i}" for i in range(3)]
    + [f"x_g{i}" for i in range(7)]
    + ["d_core"]
    + [f"d_r{i}" for i in range(7)]
    + [f"d_y{i}" for i in range(3)]
    + [f"d_z{i}" for i in range(3)]
    + [f"d_a{i}" for i in range(7)]
    + [f"d_g{i}" for i in range(7)]
    + ["c_x2b", "c_zx2b", "m_2b"]
)
INDEX = {name: i for i, name in enumerate(NAMES)}


def kernel(
    sw, bp, pw, lp, dg, g_hbm, dens, diag,
    graw, ga, mc, mr, pmat, accr, acci, xs, xy, bacc, rx, xh, ry, xu, rz, xz, outb,
    dbuf, dr0, d1, drow, d2, dy, d3, dz, dfin, d4,
    gsem, ssem, rsem,
):
    p, r, c = lax.axis_index("pole"), lax.axis_index("row"), lax.axis_index("col")
    x, zl = lax.rem(r, 4), lax.div(r, 4)
    h, k = lax.div(c, 2), lax.rem(c, 2)
    up, down, far = lax.rem(x + 1, 4), lax.rem(x + 3, 4), lax.rem(x + 2, 4)
    other = (1 - zl) * 4
    here = zl * 4
    rp, rm, r2 = here + up, here + down, here + far
    rz0, rzp, rzm, rz2 = other + x, other + up, other + down, other + far
    hp, hm, h2 = lax.rem(h + 1, 4), lax.rem(h + 3, 4), lax.rem(h + 2, 4)
    partner = h * 2 + 1 - k

    rows = []
    for dz_ in range(2):
        for dx in range(4):
            if (dz_, dx) != (0, 0):
                rows.append(lax.rem(zl + dz_, 2) * 4 + lax.rem(x + dx, 4))
    poles = [lax.rem(p + i, 4) for i in range(1, 4)]
    spans = [lax.rem(h + i, 4) for i in range(1, 4)]
    mates = [(p, partner)] + [(q, cc) for q in poles for cc in (c, partner)]

    def copy(name, src, dst, target, arrive=None):
        i = INDEX[name]
        j = INDEX[arrive or name]
        return pltpu.make_async_remote_copy(
            src_ref=src, dst_ref=dst, send_sem=ssem.at[i], recv_sem=rsem.at[j],
            device_id=target, device_id_type=MESH,
        )

    reads = [pltpu.make_async_copy(g_hbm.at[i], graw.at[i], gsem.at[i]) for i in range(2)]
    for read in reads:
        read.start()

    barrier = pltpu.get_barrier_semaphore()
    peers = [(p, rr, c) for rr in rows] + [(p, r, hh * 2 + k) for hh in spans] + [(q, r, cc) for q, cc in mates]
    for peer in peers:
        pl.semaphore_signal(barrier, inc=1, device_id=peer, device_id_type=MESH)

    widths = [sw[i] for i in range(4)]
    starts = [0 * widths[0], widths[0], widths[0] + widths[1], widths[0] + widths[1] + widths[2]]

    def pick(values, which):
        out = jnp.where(which == 0, values[0], values[1])
        out = jnp.where(which == 2, values[2], out)
        return jnp.where(which == 3, values[3], out)

    slot = lax.broadcasted_iota(jnp.int32, (1, 512), 1)
    node, inner = slot // 128, slot % 128
    kept = (inner < pick(widths, node)) & (pick([bp[0, i] for i in range(4)], node) == 1)
    place = jnp.where(kept, pick(starts, node) + inner, -1)
    line = lax.broadcasted_iota(jnp.int32, (PACKED, 512), 0)
    chooser = jnp.where(line == place, 1.0, 0.0).astype(BF16)
    for part in range(2):
        own = nt(chooser, lp[part]).astype(BF16)
        mc[r, part] = own
        mr[c, part] = own

    pl.semaphore_wait(barrier, len(peers))

    mine, own_r = mc.at[r], mr.at[c]
    c_z = copy("c_z", mine, mine, (p, rz0, c))
    c_xp = copy("c_xp", mine, mine, (p, rp, c))
    c_xm = copy("c_xm", mine, mine, (p, rm, c))
    m_p = copy("m_p", own_r, own_r, (p, r, hp * 2 + k))
    m_m = copy("m_m", own_r, own_r, (p, r, hm * 2 + k))
    m_k0 = copy("m_k0", own_r, own_r, (p, r, partner))
    for started in (c_z, c_xp, c_xm, m_p, m_m, m_k0):
        started.start()

    srow = lax.broadcasted_iota(jnp.int32, (512, 1), 0)
    rnode, rinner = srow // 128, srow % 128
    rplace = jnp.where(rinner < pick(widths, rnode), pick(starts, rnode) + rinner, -1)
    across = lax.broadcasted_iota(jnp.int32, (512, PACKED), 1)
    pmat[...] = jnp.where(across == rplace, 1.0, 0.0).astype(BF16)

    def relayout(part):
        reads[part].wait()

        @pl.loop(0, 32)
        def _(i):
            at = pl.multiple_of(i * 32, 32)
            block = graw[part, pl.ds(at, 32)]
            turned = jnp.swapaxes(block.astype(F32), 0, 1).astype(BF16)
            ga[:, pl.ds(at, 32), part * 128 : part * 128 + 128] = turned

    relayout(0)

    c_xp.wait_recv()
    c_x2 = copy("c_x2", mc.at[rm, 0], mc.at[rm, 0], (p, rp, c))
    c_x2.start()
    c_xm.wait_recv()
    c_x2b = copy("c_x2b", mc.at[rp, 1], mc.at[rp, 1], (p, rm, c), "c_x2")
    c_x2b.start()
    c_z.wait_recv()
    c_zxp = copy("c_zxp", mc.at[rz0], mc.at[rz0], (p, rp, c))
    c_zxm = copy("c_zxm", mc.at[rz0], mc.at[rz0], (p, rm, c))
    c_zxp.start()
    c_zxm.start()

    relayout(1)

    accr[...] = jnp.zeros_like(accr)
    acci[...] = jnp.zeros_like(acci)

    def multiply(a):
        real, imag = mc[a, 0], mc[a, 1]
        right = ga[a]
        accr[...] += nt(jnp.concatenate([real, -imag], axis=1), right)
        acci[...] += nt(jnp.concatenate([imag, real], axis=1), right)

    @pl.loop(0, 4)
    def _(i):
        multiply(jnp.where(i == 0, r, jnp.where(i == 1, rm, jnp.where(i == 2, rp, rz0))))

    c_zxp.wait_recv()
    c_zx2 = copy("c_zx2", mc.at[rzm, 0], mc.at[rzm, 0], (p, rp, c))
    c_zx2.start()
    c_zxm.wait_recv()
    c_zx2b = copy("c_zx2b", mc.at[rzp, 1], mc.at[rzp, 1], (p, rm, c), "c_zx2")
    c_zx2b.start()

    m_p.wait_recv()
    bm, bp_, b2 = hm * 2 + k, hp * 2 + k, h2 * 2 + k
    m_2 = copy("m_2", mr.at[bm, 0], mr.at[bm, 0], (p, r, bp_))
    m_2.start()
    m_k1 = copy("m_k1", mr.at[bm], mr.at[bm], (p, r, partner))
    m_k1.start()
    m_m.wait_recv()
    m_2b = copy("m_2b", mr.at[bp_, 1], mr.at[bp_, 1], (p, r, bm), "m_2")
    m_2b.start()
    m_k2 = copy("m_k2", mr.at[bp_], mr.at[bp_], (p, r, partner))
    m_k2.start()

    copy("c_x2", mc.at[r2], mc.at[r2], (p, rp, c)).wait_recv()

    @pl.loop(0, 3)
    def _(i):
        multiply(jnp.where(i == 0, rzm, jnp.where(i == 1, rzp, r2)))

    copy("c_zx2", mc.at[rz2], mc.at[rz2], (p, rp, c)).wait_recv()
    multiply(rz2)

    w_real, w_imag = pw[0, 0], pw[0, 1]
    for b in range(8):
        lanes = slice(b * 128, b * 128 + 128)
        real, imag = accr[:, lanes], acci[:, lanes]
        xv = w_real * real - w_imag * imag
        yv = w_real * imag + w_imag * real
        xs[b // 4, b % 4] = xv
        xh_, xl_ = split(xv)
        yh_, yl_ = split(yv)
        xy[b] = jnp.concatenate([xh_, yh_, xl_, yl_], axis=1)

    x_core = copy("x_core", xs.at[1 - k], rx, (p, r, partner))
    x_core.start()

    copy("m_2", mr.at[b2], mr.at[b2], (p, r, partner)).wait_recv()
    m_k3 = copy("m_k3", mr.at[b2], mr.at[b2], (p, r, partner))
    m_k3.start()

    x_core.wait_recv()
    for q in range(4):
        xh[q] = xs[k, q] + rx[q]
    x_y = [copy(f"x_y{i}", xh.at[q], ry.at[i], (q, r, c)) for i, q in enumerate(poles)]
    for started in x_y:
        started.start()

    for arrived in (m_k0, m_k1, m_k2, m_k3):
        arrived.wait_recv()
    bacc[...] = jnp.zeros_like(bacc)

    @pl.loop(0, 8)
    def _(b):
        real, imag = mr[b, 0], mr[b, 1]
        left = jnp.concatenate([real, -imag, real, -imag], axis=1)
        bacc[...] += nt(left, xy[b])

    high, low = split(bacc[...])
    tall = nn(pmat[...], high) + nn(pmat[...], low)
    lead = jnp.where((r == 0) & (c == 0), 1.0, 0.0)
    for node_ in range(4):
        band = slice(node_ * 128, node_ * 128 + 128)
        high, low = split(tall[band])
        chosen = pmat[band]
        own_term = w_real * dg[0, band].astype(F32) - w_imag * dg[1, band].astype(F32)
        term = nt(high, chosen) + nt(low, chosen) + lead * own_term
        dbuf[node_ // 2, (node_ % 2) * 2 : (node_ % 2) * 2 + 2] = term.reshape(2, 8, 8, 128)

    d_core = copy("d_core", dbuf.at[1 - k], dr0, (p, r, partner))
    d_core.start()
    d_core.wait_recv()
    d1[...] = dbuf[k] + dr0[...]
    d_r = [copy(f"d_r{i}", d1.at[:, rr], drow.at[i], (p, rr, c)) for i, rr in enumerate(rows)]
    for started in d_r:
        started.start()
    for arrived in d_r:
        arrived.wait_recv()
    d2[...] = d1[:, r] + ((drow[0] + drow[1]) + (drow[2] + drow[3])) + ((drow[4] + drow[5]) + drow[6])
    d_y = [copy(f"d_y{i}", d2.at[q], dy.at[i], (q, r, c)) for i, q in enumerate(poles)]
    for started in d_y:
        started.start()

    for arrived in x_y:
        arrived.wait_recv()
    high, low = split(-((xh[p] + ry[0]) + (ry[1] + ry[2])))
    xu[...] = (nn(pmat[...], high) + nn(pmat[...], low)).reshape(4, 128, 128)

    for arrived in d_y:
        arrived.wait_recv()
    d3[...] = (d2[p] + dy[0]) + (dy[1] + dy[2])
    dz[h] = d3[...]
    d_z = [copy(f"d_z{i}", d3, dz.at[h], (p, r, hh * 2 + k)) for i, hh in enumerate(spans)]
    for started in d_z:
        started.start()
    x_z = [copy(f"x_z{i}", xu.at[hh], rz.at[i], (p, r, hh * 2 + k)) for i, hh in enumerate(spans)]
    for started in x_z:
        started.start()

    for arrived in d_z:
        arrived.wait_recv()
    total = (dz[0] + dz[1]) + (dz[2] + dz[3])
    d4[...] = total
    dfin[k, p, r] = total
    d_a = [copy(f"d_a{i}", d4, dfin.at[k, p, r], (p, rr, c)) for i, rr in enumerate(rows)]
    for started in d_a:
        started.start()

    for arrived in x_z:
        arrived.wait_recv()
    xz[...] = ((xu[h] + rz[0]) + (rz[1] + rz[2])).reshape(2, 64, 128)
    spot = k * 4 + p
    outb[spot] = xz[k]
    x_g = [
        copy(f"x_g{i}", xz.at[lax.rem(cc, 2)], outb.at[spot], (q, r, cc)) for i, (q, cc) in enumerate(mates)
    ]
    for started in x_g:
        started.start()

    for arrived in d_a:
        arrived.wait_recv()
    d_g = [copy(f"d_g{i}", dfin.at[k, p], dfin.at[k, p], (q, r, cc)) for i, (q, cc) in enumerate(mates)]
    for started in d_g:
        started.start()

    for arrived in x_g:
        arrived.wait_recv()
    for b in range(8):
        dens[:, b * 128 : b * 128 + 128] = outb[b]
    for arrived in d_g:
        arrived.wait_recv()
    diag[...] = dfin[...].reshape(512, 128)

    sent = [c_z, c_xp, c_xm, c_x2, c_x2b, c_zxp, c_zxm, c_zx2, c_zx2b, m_p, m_m, m_2, m_2b]
    sent += [m_k0, m_k1, m_k2, m_k3, x_core, d_core]
    sent += x_y + x_z + x_g + d_r + d_y + d_z + d_a + d_g
    for done in sent:
        done.wait_send()


def per_device(found_inverse, l_panel, block_pattern, sup_widths, diag_inverse, pole_weights):
    vmem = pl.BlockSpec(memory_space=pltpu.VMEM)
    smem = pl.BlockSpec(memory_space=pltpu.SMEM)
    n = len(NAMES)
    V = pltpu.VMEM
    return pl.pallas_call(
        kernel,
        out_shape=(jax.ShapeDtypeStruct((64, 1024), F32), jax.ShapeDtypeStruct((512, 128), F32)),
        in_specs=[smem, smem, smem, vmem, vmem, pl.BlockSpec(memory_space=pl.ANY)],
        out_specs=(vmem, vmem),
        scratch_shapes=[
            V((2, 1024, 8, 128), BF16),
            V((8, 1024, 256), BF16),
            V((8, 2, PACKED, 128), BF16),
            V((8, 2, PACKED, 128), BF16),
            V((512, PACKED), BF16),
            V((PACKED, 1024), F32),
            V((PACKED, 1024), F32),
            V((2, 4, PACKED, 128), F32),
            V((8, PACKED, 512), BF16),
            V((PACKED, PACKED), F32),
            V((4, PACKED, 128), F32),
            V((4, PACKED, 128), F32),
            V((3, PACKED, 128), F32),
            V((4, 128, 128), F32),
            V((3, 128, 128), F32),
            V((2, 64, 128), F32),
            V((8, 64, 128), F32),
            V((2, 4, 8, 8, 128), F32),
            V((4, 8, 8, 128), F32),
            V((4, 8, 8, 128), F32),
            V((7, 4, 8, 128), F32),
            V((4, 8, 128), F32),
            V((3, 8, 128), F32),
            V((8, 128), F32),
            V((4, 8, 128), F32),
            V((2, 4, 8, 8, 128), F32),
            V((8, 128), F32),
            pltpu.SemaphoreType.DMA((2,)),
            pltpu.SemaphoreType.DMA((n,)),
            pltpu.SemaphoreType.DMA((n,)),
        ],
        compiler_params=pltpu.CompilerParams(
            collective_id=0, has_side_effects=True, vmem_limit_bytes=48 << 20
        ),
    )(
        sup_widths, block_pattern, pole_weights, l_panel[0], diag_inverse[0],
        found_inverse.reshape(2, 1024, 8, 128),
    )


def solution(mesh):
    in_specs = (
        P("pole", None, "row", None, "col", None),
        P("pole", None, ("row", "col"), None),
        P(("row", "col"), None),
        P(),
        P("pole", None, None, None),
        P("pole", None),
    )
    out_specs = (P("col", "row"), P())
    return jax.shard_map(
        per_device, mesh=mesh, in_specs=in_specs, out_specs=out_specs, check_vma=False
    )
```

```python
import functools

import jax
import jax.numpy as jnp
from jax import lax
from jax.experimental import pallas as pl
from jax.experimental.pallas import tpu as pltpu
from jax.sharding import PartitionSpec as P

MESH = pl.DeviceIdType.MESH
PACKED = 320
F32, BF16 = jnp.float32, jnp.bfloat16


def nt(left, right):
    return lax.dot_general(left, right, (((1,), (1,)), ((), ())), preferred_element_type=F32)


def nn(left, right):
    return lax.dot_general(left, right, (((1,), (0,)), ((), ())), preferred_element_type=F32)


def split(value):
    high = value.astype(BF16)
    return high, (value - high.astype(F32)).astype(BF16)


HALF = PACKED // 2
NAMES = [
    f"{name}_{half}"
    for half in range(2)
    for name in (
        ["c_z", "c_xp", "c_xm", "c_zxp", "c_zxm", "c_x2", "c_x2b", "c_zx2", "c_zx2b"]
        + [f"c_k{i}" for i in range(8)]
        + [f"x_y{i}" for i in range(3)]
        + [f"x_z{i}" for i in range(3)]
    )
]
NAMES += ["g_0", "g_1", "m_p", "m_m", "m_k"] + [f"x_a{i}" for i in range(4)] + [f"x_b{i}" for i in range(3)]
NAMES += ["d_core"] + [f"d_r{i}" for i in range(7)] + [f"d_y{i}" for i in range(3)]
NAMES += [f"d_z{i}" for i in range(3)] + [f"d_a{i}" for i in range(7)] + [f"d_g{i}" for i in range(7)]
INDEX = {name: i for i, name in enumerate(NAMES)}


def kernel(
    sw_hbm, bp_hbm, pw_hbm, lp_hbm, dg_hbm, g_hbm, dens, diag,
    sw, bp, pw, lp, dg, graw, ga, own, mc, mr, pmat, acc, xs, xy, bacc, ry, xu, rz, xz, outb,
    dbuf, dr0, d1, drow, d2, dy, d3, dz, dfin, d4,
    gsem, ssem, rsem, mssem, mrsem,
):
    p, r, c = lax.axis_index("pole"), lax.axis_index("row"), lax.axis_index("col")
    x, zl = lax.rem(r, 4), lax.div(r, 4)
    h, k = lax.div(c, 2), lax.rem(c, 2)
    up, down, far = lax.rem(x + 1, 4), lax.rem(x + 3, 4), lax.rem(x + 2, 4)
    other = (1 - zl) * 4
    here = zl * 4
    rp, rm, r2 = here + up, here + down, here + far
    rz0, rzp, rzm, rz2 = other + x, other + up, other + down, other + far
    hp, hm = lax.rem(h + 1, 4), lax.rem(h + 3, 4)
    partner = h * 2 + 1 - k
    side = lax.div(h, 2)

    rows = []
    for dz_ in range(2):
        for dx in range(4):
            if (dz_, dx) != (0, 0):
                rows.append(lax.rem(zl + dz_, 2) * 4 + lax.rem(x + dx, 4))
    poles = [lax.rem(p + i, 4) for i in range(1, 4)]
    spans = [lax.rem(h + i, 4) for i in range(1, 4)]
    mates = [(p, partner)] + [(q, cc) for q in poles for cc in (c, partner)]

    def copy(name, src, dst, target, arrive=None):
        i = INDEX[name]
        j = INDEX[arrive or name]
        return pltpu.make_async_remote_copy(
            src_ref=src, dst_ref=dst, send_sem=ssem.at[i], recv_sem=rsem.at[j],
            device_id=target, device_id_type=MESH,
        )

    sent = []

    def start(*copies):
        for each in copies:
            each.start()
            sent.append(each)

    small = [
        pltpu.make_async_copy(src, dst, gsem.at[2 + i])
        for i, (src, dst) in enumerate([(sw_hbm, sw), (bp_hbm, bp), (lp_hbm, lp), (pw_hbm, pw), (dg_hbm, dg)])
    ]
    for read in small:
        read.start()
    near = pl.ds(pl.multiple_of(k * 512, 512), 512)
    away = pl.ds(pl.multiple_of((1 - k) * 512, 512), 512)
    reads = [pltpu.make_async_copy(g_hbm.at[i, near], graw.at[k, i], gsem.at[i]) for i in range(2)]
    for read in reads:
        read.start()

    barrier = pltpu.get_barrier_semaphore()
    peers = [(p, rr, c) for rr in rows] + [(p, r, hh * 2 + k) for hh in spans] + [(q, r, cc) for q, cc in mates]
    peers += [(p, r, hh * 2 + 1 - k) for hh in (hp, hm)]
    for peer in peers:
        pl.semaphore_signal(barrier, inc=1, device_id=peer, device_id_type=MESH)

    for read in small[:3]:
        read.wait()
    widths = [sw[i] for i in range(4)]
    starts = [0 * widths[0], widths[0], widths[0] + widths[1], widths[0] + widths[1] + widths[2]]

    def pick(values, which):
        out = jnp.where(which == 0, values[0], values[1])
        out = jnp.where(which == 2, values[2], out)
        return jnp.where(which == 3, values[3], out)

    slot = lax.broadcasted_iota(jnp.int32, (1, 512), 1)
    node, inner = slot // 128, slot % 128
    kept = (inner < pick(widths, node)) & (pick([bp[0, i] for i in range(4)], node) == 1)
    place = jnp.where(kept, pick(starts, node) + inner, -1)
    line = lax.broadcasted_iota(jnp.int32, (PACKED, 512), 0)
    chooser = jnp.where(line == place, 1.0, 0.0).astype(BF16)
    seat = lax.rem(h, 2) * 2 + k
    for part in range(2):
        packed = nt(chooser, lp[part]).astype(BF16)
        own[part] = packed
        for half in range(2):
            mc[half, k, r, part] = packed[half * HALF : half * HALF + HALF]

    @pl.when(side == k)
    def _():
        mr[seat] = own[...]

    pl.semaphore_wait(barrier, len(peers))

    def row(rr):
        return (p, rr, c)

    mate = (p, r, partner)
    for half in range(2):
        mine = mc.at[half, k, r]
        start(
            copy(f"c_z_{half}", mine, mine, row(rz0)),
            copy(f"c_xp_{half}", mine, mine, row(rp)),
            copy(f"c_xm_{half}", mine, mine, row(rm)),
            copy(f"c_k0_{half}", mine, mine, mate),
        )
    start(*[copy(f"g_{i}", g_hbm.at[i, away], graw.at[k, i], mate) for i in range(2)])

    def row_copy(i, target):
        return pltpu.make_async_remote_copy(
            src_ref=own, dst_ref=mr.at[seat], send_sem=ssem.at[INDEX[i]], recv_sem=mrsem.at[seat],
            device_id=(p, r, target), device_id_type=MESH,
        )

    def start_rows():
        start(row_copy("m_p", hp * 2 + side), row_copy("m_m", hm * 2 + side))

        @pl.when(side != k)
        def _():
            row_copy("m_k", partner).start()

    srow = lax.broadcasted_iota(jnp.int32, (512, 1), 0)
    rnode, rinner = srow // 128, srow % 128
    rplace = jnp.where(rinner < pick(widths, rnode), pick(starts, rnode) + rinner, -1)
    across = lax.broadcasted_iota(jnp.int32, (512, PACKED), 1)
    pmat[...] = jnp.where(across == rplace, 1.0, 0.0).astype(BF16)
    acc[...] = jnp.zeros_like(acc)

    def relayout(core, part):
        at = pl.multiple_of((core * 2 + part) * 128, 128)

        @pl.loop(0, 16)
        def _(i):
            band = pl.ds(pl.multiple_of(i * 32, 32), 32)
            block = graw[core, part, band]
            ga[:, band, pl.ds(at, 128)] = jnp.swapaxes(block.astype(F32), 0, 1).astype(BF16)

    for part in range(2):
        reads[part].wait()
        relayout(k, part)

    def arrive(name, half, block):
        ref = mc.at[half, k, block]
        copy(f"{name}_{half}", ref, ref, mate).wait_recv()

    def hand(i, half, block):
        ref = mc.at[half, k, block]
        start(copy(f"c_k{i}_{half}", ref, ref, mate))

    def first(half):
        arrive("c_xp", half, rm)
        ref = mc.at[half, k, rm, 0]
        start(copy(f"c_x2_{half}", ref, ref, row(rp)))
        arrive("c_xm", half, rp)
        ref = mc.at[half, k, rp, 1]
        start(copy(f"c_x2b_{half}", ref, ref, row(rm), f"c_x2_{half}"))
        arrive("c_z", half, rz0)
        ref = mc.at[half, k, rz0]
        start(copy(f"c_zxp_{half}", ref, ref, row(rp)), copy(f"c_zxm_{half}", ref, ref, row(rm)))
        for i, block in ((1, rm), (2, rp), (3, rz0)):
            hand(i, half, block)

    def second(half):
        arrive("c_zxp", half, rzm)
        ref = mc.at[half, k, rzm, 0]
        start(copy(f"c_zx2_{half}", ref, ref, row(rp)))
        arrive("c_zxm", half, rzp)
        ref = mc.at[half, k, rzp, 1]
        start(copy(f"c_zx2b_{half}", ref, ref, row(rm), f"c_zx2_{half}"))
        arrive("c_x2", half, r2)
        for i, block in ((4, rzm), (5, rzp), (6, r2)):
            hand(i, half, block)

    def third(half):
        arrive("c_zx2", half, rz2)
        hand(7, half, rz2)

    def handed(half, which):
        for i, block in which:
            ref = mc.at[half, 1 - k, block]
            copy(f"c_k{i}_{half}", ref, ref, mate).wait_recv()

    def multiply(half, a):
        r0, i0, r1, i1 = mc[half, 0, a, 0], mc[half, 0, a, 1], mc[half, 1, a, 0], mc[half, 1, a, 1]
        right = ga[a]
        acc[half, 0] += nt(jnp.concatenate([r0, -i0, r1, -i1], axis=1), right)
        acc[half, 1] += nt(jnp.concatenate([i0, r0, i1, r1], axis=1), right)

    def early(half):
        handed(half, ((0, r), (1, rm), (2, rp), (3, rz0)))

        @pl.loop(0, 4)
        def _(i):
            multiply(half, jnp.where(i == 0, r, jnp.where(i == 1, rm, jnp.where(i == 2, rp, rz0))))

    def middle(half):
        handed(half, ((4, rzm), (5, rzp), (6, r2)))

        @pl.loop(0, 3)
        def _(i):
            multiply(half, jnp.where(i == 0, rzm, jnp.where(i == 1, rzp, r2)))

    def late(half):
        handed(half, ((7, rz2),))
        multiply(half, rz2)

    def weigh(half):
        w_real, w_imag = pw[0, 0], pw[0, 1]
        for q in range(4):
            lanes = slice(q * 128, q * 128 + 128)
            real, imag = acc[half, 0, :, lanes], acc[half, 1, :, lanes]
            xv = w_real * real - w_imag * imag
            xs[half, q] = xv
        out = [copy(f"x_y{i}_{half}", xs.at[half, q], ry.at[half, i], (q, r, c)) for i, q in enumerate(poles)]
        start(*out)
        for q in range(4):
            lanes = slice(q * 128, q * 128 + 128)
            real, imag = acc[half, 0, :, lanes], acc[half, 1, :, lanes]
            xh_, xl_ = split(w_real * real - w_imag * imag)
            yh_, yl_ = split(w_real * imag + w_imag * real)
            xy[q, half * HALF : half * HALF + HALF] = jnp.concatenate([xh_, yh_, xl_, yl_], axis=1)
        return out

    def seat_wait(s):
        pltpu.make_async_remote_copy(
            src_ref=mr.at[s], dst_ref=mr.at[s], send_sem=mssem.at[s], recv_sem=mrsem.at[s],
            device_id=mate, device_id_type=MESH,
        ).wait_recv()

    def seat_pass(s, part, target):
        return pltpu.make_async_remote_copy(
            src_ref=mr.at[s, part], dst_ref=mr.at[s, part], send_sem=mssem.at[s], recv_sem=mrsem.at[s],
            device_id=(p, r, target * 2 + k), device_id_type=MESH,
        )

    steps = [lax.rem(2 * k + s // 2 - h + 4, 4) for s in range(4)]

    def pass_rows():
        for s in range(4):

            @pl.when(steps[s] == 3)
            def _():
                seat_wait(s)
                seat_pass(s, 0, hp).start()

            @pl.when(steps[s] == 1)
            def _():
                seat_wait(s)
                seat_pass(s, 1, hm).start()

    first(0)
    start_rows()
    for part in range(2):
        copy(f"g_{part}", graw.at[1 - k, part], graw.at[1 - k, part], mate).wait_recv()
        relayout(1 - k, part)
    first(1)
    early(0)
    second(0)
    early(1)
    second(1)
    middle(0)
    third(0)
    for read in small[3:]:
        read.wait()
    pass_rows()
    late(0)
    x_y = [weigh(0)]
    middle(1)
    third(1)
    late(1)
    x_y.append(weigh(1))

    for s in range(4):

        @pl.when((steps[s] == 2) | ((steps[s] == 0) & (s % 2 != k)))
        def _():
            seat_wait(s)

    bacc[...] = jnp.zeros_like(bacc)

    @pl.loop(0, 4)
    def _(b):
        real, imag = mr[b, 0], mr[b, 1]
        left = jnp.concatenate([real, -imag, real, -imag], axis=1)
        bacc[...] += nt(left, xy[b])

    w_real, w_imag = pw[0, 0], pw[0, 1]
    high, low = split(bacc[...])
    tall = nn(pmat[...], high) + nn(pmat[...], low)
    lead = jnp.where((r == 0) & (c == 0), 1.0, 0.0)
    for node_ in range(4):
        band = slice(node_ * 128, node_ * 128 + 128)
        high, low = split(tall[band])
        chosen = pmat[band]
        own_term = w_real * dg[0, band].astype(F32) - w_imag * dg[1, band].astype(F32)
        term = nt(high, chosen) + nt(low, chosen) + lead * own_term
        dbuf[node_ // 2, (node_ % 2) * 2 : (node_ % 2) * 2 + 2] = term.reshape(2, 8, 8, 128)

    d_core = copy("d_core", dbuf.at[1 - k], dr0, mate)
    start(d_core)
    d_core.wait_recv()
    d1[...] = dbuf[k] + dr0[...]
    d_r = [copy(f"d_r{i}", d1.at[:, rr], drow.at[i], row(rr)) for i, rr in enumerate(rows)]
    start(*d_r)

    for arrived in x_y[0] + x_y[1]:
        arrived.wait_recv()
    halves = [-((xs[half, p] + ry[half, 0]) + (ry[half, 1] + ry[half, 2])) for half in range(2)]
    high, low = split(jnp.concatenate(halves, axis=0))
    xu[...] = (nn(pmat[...], high) + nn(pmat[...], low)).reshape(4, 2, 64, 128)
    x_z = []
    for turn, which in enumerate((1 - k, k)):
        x_z.append(
            [
                copy(f"x_z{i}_{turn}", xu.at[hh, which], rz.at[turn, i], (p, r, hh * 2 + k))
                for i, hh in enumerate(spans)
            ]
        )

    for arrived in d_r:
        arrived.wait_recv()
    d2[...] = d1[:, r] + ((drow[0] + drow[1]) + (drow[2] + drow[3])) + ((drow[4] + drow[5]) + drow[6])
    d_y = [copy(f"d_y{i}", d2.at[q], dy.at[i], (q, r, c)) for i, q in enumerate(poles)]
    start(*d_y)
    start(*x_z[0], *x_z[1])

    for arrived in d_y:
        arrived.wait_recv()
    d3[...] = (d2[p] + dy[0]) + (dy[1] + dy[2])
    dz[h] = d3[...]
    d_z = [copy(f"d_z{i}", d3, dz.at[h], (p, r, hh * 2 + k)) for i, hh in enumerate(spans)]
    start(*d_z)

    spot = k * 4 + p
    for arrived in x_z[0]:
        arrived.wait_recv()
    xz[0] = (xu[h, 1 - k] + rz[0, 0]) + (rz[0, 1] + rz[0, 2])
    x_a = [copy(f"x_a{i}", xz.at[0], outb.at[spot], (q, r, partner)) for i, q in enumerate([p] + poles)]
    start(*x_a)

    for arrived in d_z:
        arrived.wait_recv()
    total = (dz[0] + dz[1]) + (dz[2] + dz[3])
    d4[...] = total
    dfin[k, p, r] = total
    d_a = [copy(f"d_a{i}", d4, dfin.at[k, p, r], row(rr)) for i, rr in enumerate(rows)]
    start(*d_a)

    for arrived in x_z[1]:
        arrived.wait_recv()
    xz[1] = (xu[h, k] + rz[1, 0]) + (rz[1, 1] + rz[1, 2])
    outb[spot] = xz[1]
    x_b = [copy(f"x_b{i}", xz.at[1], outb.at[spot], (q, r, c)) for i, q in enumerate(poles)]
    start(*x_b)

    for arrived in d_a:
        arrived.wait_recv()
    d_g = [copy(f"d_g{i}", dfin.at[k, p], dfin.at[k, p], (q, r, cc)) for i, (q, cc) in enumerate(mates)]
    start(*d_g)

    for arrived in x_a + x_b:
        arrived.wait_recv()
    for b in range(8):
        dens[:, b * 128 : b * 128 + 128] = outb[b]
    for arrived in d_g:
        arrived.wait_recv()
    diag[...] = dfin[...].reshape(512, 128)

    for done in sent:
        done.wait_send()

    @pl.when(side != k)
    def _():
        row_copy("m_k", partner).wait_send()

    for s in range(4):

        @pl.when((steps[s] == 3) | (steps[s] == 1))
        def _():
            seat_pass(s, 0, hp).wait_send()


def per_device(found_inverse, l_panel, block_pattern, sup_widths, diag_inverse, pole_weights):
    vmem = pl.BlockSpec(memory_space=pltpu.VMEM)
    n = len(NAMES)
    V = pltpu.VMEM
    return pl.pallas_call(
        kernel,
        out_shape=(jax.ShapeDtypeStruct((64, 1024), F32), jax.ShapeDtypeStruct((512, 128), F32)),
        in_specs=[pl.BlockSpec(memory_space=pltpu.MemorySpace.HBM)] * 6,
        out_specs=(vmem, vmem),
        scratch_shapes=[
            pltpu.SMEM((4,), jnp.int32),
            pltpu.SMEM((1, 4), jnp.int32),
            pltpu.SMEM((1, 2), F32),
            V((2, 128, 512), BF16),
            V((2, 512, 128), BF16),
            V((2, 2, 512, 8, 128), BF16),
            V((8, 512, 512), BF16),
            V((2, PACKED, 128), BF16),
            V((2, 2, 8, 2, HALF, 128), BF16),
            V((4, 2, PACKED, 128), BF16),
            V((512, PACKED), BF16),
            V((2, 2, HALF, 512), F32),
            V((2, 4, HALF, 128), F32),
            V((4, PACKED, 512), BF16),
            V((PACKED, PACKED), F32),
            V((2, 3, HALF, 128), F32),
            V((4, 2, 64, 128), F32),
            V((2, 3, 64, 128), F32),
            V((2, 64, 128), F32),
            V((8, 64, 128), F32),
            V((2, 4, 8, 8, 128), F32),
            V((4, 8, 8, 128), F32),
            V((4, 8, 8, 128), F32),
            V((7, 4, 8, 128), F32),
            V((4, 8, 128), F32),
            V((3, 8, 128), F32),
            V((8, 128), F32),
            V((4, 8, 128), F32),
            V((2, 4, 8, 8, 128), F32),
            V((8, 128), F32),
            pltpu.SemaphoreType.DMA((7,)),
            pltpu.SemaphoreType.DMA((n,)),
            pltpu.SemaphoreType.DMA((n,)),
            pltpu.SemaphoreType.DMA((4,)),
            pltpu.SemaphoreType.DMA((4,)),
        ],
        compiler_params=pltpu.CompilerParams(
            collective_id=0, has_side_effects=True, vmem_limit_bytes=65500000
        ),
    )(
        sup_widths, block_pattern, pole_weights, l_panel[0], diag_inverse[0],
        found_inverse.reshape(2, 1024, 8, 128),
    )


def solution(mesh):
    in_specs = (
        P("pole", None, "row", None, "col", None),
        P("pole", None, ("row", "col"), None),
        P(("row", "col"), None),
        P(),
        P("pole", None, None, None),
        P("pole", None),
    )
    out_specs = (P("col", "row"), P())
    return jax.shard_map(
        per_device, mesh=mesh, in_specs=in_specs, out_specs=out_specs, check_vma=False
    )
```

```python
import functools

import jax
import jax.numpy as jnp
from jax import lax
from jax.experimental import pallas as pl
from jax.experimental.pallas import tpu as pltpu
from jax.sharding import PartitionSpec as P

MESH = pl.DeviceIdType.MESH
PACKED = 320
F32, BF16 = jnp.float32, jnp.bfloat16


def nt(left, right):
    return lax.dot_general(left, right, (((1,), (1,)), ((), ())), preferred_element_type=F32)


def nn(left, right):
    return lax.dot_general(left, right, (((1,), (0,)), ((), ())), preferred_element_type=F32)


def split(value):
    high = value.astype(BF16)
    return high, (value - high.astype(F32)).astype(BF16)


HALF = PACKED // 2
NAMES = [
    f"{name}_{half}"
    for half in range(2)
    for name in (
        ["c_z", "c_xp", "c_xm", "c_zxp", "c_zxm", "c_x2", "c_x2b", "c_zx2", "c_zx2b"]
        + [f"c_k{i}" for i in range(8)]
        + [f"x_y{i}" for i in range(3)]
        + [f"x_z{i}" for i in range(3)]
    )
]
NAMES += ["g_0", "g_1", "m_p", "m_m", "m_k"] + [f"x_a{i}" for i in range(4)] + [f"x_b{i}" for i in range(3)]
NAMES += ["d_core", "d_c"] + [f"d_r{i}" for i in range(7)] + [f"d_s{i}" for i in range(15)]
NAMES += [f"d_p{i}" for i in range(3)] + [f"d_a{i}" for i in range(7)]
INDEX = {name: i for i, name in enumerate(NAMES)}


def kernel(
    sw_hbm, bp_hbm, pw_hbm, lp_hbm, dg_hbm, g_hbm, dens, diag,
    sw, bp, pw, lp, dg, graw, ga, own, mc, mr, pmat, acc, xs, xy, bacc, ry, xu, rz, xz, outb,
    dbuf, dr0, d1, drow, d2, ds, dfin,
    gsem, ssem, rsem, mssem, mrsem,
):
    p, r, c = lax.axis_index("pole"), lax.axis_index("row"), lax.axis_index("col")
    x, zl = lax.rem(r, 4), lax.div(r, 4)
    h, k = lax.div(c, 2), lax.rem(c, 2)
    up, down, far = lax.rem(x + 1, 4), lax.rem(x + 3, 4), lax.rem(x + 2, 4)
    other = (1 - zl) * 4
    here = zl * 4
    rp, rm, r2 = here + up, here + down, here + far
    rz0, rzp, rzm, rz2 = other + x, other + up, other + down, other + far
    hp, hm = lax.rem(h + 1, 4), lax.rem(h + 3, 4)
    partner = h * 2 + 1 - k
    side = lax.div(h, 2)

    rows = []
    for dz_ in range(2):
        for dx in range(4):
            if (dz_, dx) != (0, 0):
                rows.append(lax.rem(zl + dz_, 2) * 4 + lax.rem(x + dx, 4))
    poles = [lax.rem(p + i, 4) for i in range(1, 4)]
    spans = [lax.rem(h + i, 4) for i in range(1, 4)]
    mates = [(p, partner)] + [(q, cc) for q in poles for cc in (c, partner)]

    def copy(name, src, dst, target, arrive=None):
        i = INDEX[name]
        j = INDEX[arrive or name]
        return pltpu.make_async_remote_copy(
            src_ref=src, dst_ref=dst, send_sem=ssem.at[i], recv_sem=rsem.at[j],
            device_id=target, device_id_type=MESH,
        )

    sent = []

    def start(*copies):
        for each in copies:
            each.start()
            sent.append(each)

    small = [
        pltpu.make_async_copy(src, dst, gsem.at[2 + i])
        for i, (src, dst) in enumerate([(sw_hbm, sw), (bp_hbm, bp), (lp_hbm, lp), (pw_hbm, pw), (dg_hbm, dg)])
    ]
    for read in small:
        read.start()
    near = pl.ds(pl.multiple_of(k * 512, 512), 512)
    away = pl.ds(pl.multiple_of((1 - k) * 512, 512), 512)
    reads = [pltpu.make_async_copy(g_hbm.at[i, near], graw.at[k, i], gsem.at[i]) for i in range(2)]
    for read in reads:
        read.start()

    barrier = pltpu.get_barrier_semaphore()
    peers = [(p, rr, c) for rr in (rp, rm, rz0)] + [(p, r, hh * 2 + k) for hh in spans]
    peers += [(q, r, c) for q in poles] + [(p, r, partner)]
    for peer in peers:
        pl.semaphore_signal(barrier, inc=1, device_id=peer, device_id_type=MESH)

    for read in small[:3]:
        read.wait()
    widths = [sw[i] for i in range(4)]
    starts = [0 * widths[0], widths[0], widths[0] + widths[1], widths[0] + widths[1] + widths[2]]

    def pick(values, which):
        out = jnp.where(which == 0, values[0], values[1])
        out = jnp.where(which == 2, values[2], out)
        return jnp.where(which == 3, values[3], out)

    slot = lax.broadcasted_iota(jnp.int32, (1, 512), 1)
    node, inner = slot // 128, slot % 128
    kept = (inner < pick(widths, node)) & (pick([bp[0, i] for i in range(4)], node) == 1)
    place = jnp.where(kept, pick(starts, node) + inner, -1)
    line = lax.broadcasted_iota(jnp.int32, (PACKED, 512), 0)
    chooser = jnp.where(line == place, 1.0, 0.0).astype(BF16)
    seat = lax.rem(h, 2) * 2 + k
    for part in range(2):
        packed = nt(chooser, lp[part]).astype(BF16)
        own[part] = packed
        for half in range(2):
            mc[half, k, r, part] = packed[half * HALF : half * HALF + HALF]

    @pl.when(side == k)
    def _():
        mr[seat] = own[...]

    pl.semaphore_wait(barrier, len(peers))

    def row(rr):
        return (p, rr, c)

    mate = (p, r, partner)
    for half in range(2):
        mine = mc.at[half, k, r]
        start(
            copy(f"c_z_{half}", mine, mine, row(rz0)),
            copy(f"c_xp_{half}", mine, mine, row(rp)),
            copy(f"c_xm_{half}", mine, mine, row(rm)),
            copy(f"c_k0_{half}", mine, mine, mate),
        )
    start(*[copy(f"g_{i}", g_hbm.at[i, away], graw.at[k, i], mate) for i in range(2)])

    def row_copy(i, target):
        return pltpu.make_async_remote_copy(
            src_ref=own, dst_ref=mr.at[seat], send_sem=ssem.at[INDEX[i]], recv_sem=mrsem.at[seat],
            device_id=(p, r, target), device_id_type=MESH,
        )

    def start_rows():
        start(row_copy("m_p", hp * 2 + side), row_copy("m_m", hm * 2 + side))

        @pl.when(side != k)
        def _():
            row_copy("m_k", partner).start()

    srow = lax.broadcasted_iota(jnp.int32, (512, 1), 0)
    rnode, rinner = srow // 128, srow % 128
    rplace = jnp.where(rinner < pick(widths, rnode), pick(starts, rnode) + rinner, -1)
    across = lax.broadcasted_iota(jnp.int32, (512, PACKED), 1)
    pmat[...] = jnp.where(across == rplace, 1.0, 0.0).astype(BF16)
    acc[...] = jnp.zeros_like(acc)

    def relayout(core, part):
        at = pl.multiple_of((core * 2 + part) * 128, 128)

        @pl.loop(0, 16)
        def _(i):
            band = pl.ds(pl.multiple_of(i * 32, 32), 32)
            block = graw[core, part, band]
            ga[:, band, pl.ds(at, 128)] = jnp.swapaxes(block.astype(F32), 0, 1).astype(BF16)

    for part in range(2):
        reads[part].wait()
        relayout(k, part)

    def arrive(name, half, block):
        ref = mc.at[half, k, block]
        copy(f"{name}_{half}", ref, ref, mate).wait_recv()

    def hand(i, half, block):
        ref = mc.at[half, k, block]
        start(copy(f"c_k{i}_{half}", ref, ref, mate))

    def first(half):
        arrive("c_xp", half, rm)
        ref = mc.at[half, k, rm, 0]
        start(copy(f"c_x2_{half}", ref, ref, row(rp)))
        arrive("c_xm", half, rp)
        ref = mc.at[half, k, rp, 1]
        start(copy(f"c_x2b_{half}", ref, ref, row(rm), f"c_x2_{half}"))
        arrive("c_z", half, rz0)
        ref = mc.at[half, k, rz0]
        start(copy(f"c_zxp_{half}", ref, ref, row(rp)), copy(f"c_zxm_{half}", ref, ref, row(rm)))
        for i, block in ((1, rm), (2, rp), (3, rz0)):
            hand(i, half, block)

    def second(half):
        arrive("c_zxp", half, rzm)
        ref = mc.at[half, k, rzm, 0]
        start(copy(f"c_zx2_{half}", ref, ref, row(rp)))
        arrive("c_zxm", half, rzp)
        ref = mc.at[half, k, rzp, 1]
        start(copy(f"c_zx2b_{half}", ref, ref, row(rm), f"c_zx2_{half}"))
        arrive("c_x2", half, r2)
        for i, block in ((4, rzm), (5, rzp), (6, r2)):
            hand(i, half, block)

    def third(half):
        arrive("c_zx2", half, rz2)
        hand(7, half, rz2)

    def handed(half, which):
        for i, block in which:
            ref = mc.at[half, 1 - k, block]
            copy(f"c_k{i}_{half}", ref, ref, mate).wait_recv()

    def multiply(half, a):
        r0, i0, r1, i1 = mc[half, 0, a, 0], mc[half, 0, a, 1], mc[half, 1, a, 0], mc[half, 1, a, 1]
        right = ga[a]
        acc[half, 0] += nt(jnp.concatenate([r0, -i0, r1, -i1], axis=1), right)
        acc[half, 1] += nt(jnp.concatenate([i0, r0, i1, r1], axis=1), right)

    def early(half):
        handed(half, ((0, r), (1, rm), (2, rp), (3, rz0))[1 - half :])

        @pl.loop(0, 4)
        def _(i):
            multiply(half, jnp.where(i == 0, r, jnp.where(i == 1, rm, jnp.where(i == 2, rp, rz0))))

    def middle(half):
        handed(half, ((4, rzm), (5, rzp), (6, r2)))

        @pl.loop(0, 3)
        def _(i):
            multiply(half, jnp.where(i == 0, rzm, jnp.where(i == 1, rzp, r2)))

    def late(half):
        handed(half, ((7, rz2),))
        multiply(half, rz2)

    def weigh(half):
        w_real, w_imag = pw[0, 0], pw[0, 1]
        for q in range(4):
            lanes = slice(q * 128, q * 128 + 128)
            real, imag = acc[half, 0, :, lanes], acc[half, 1, :, lanes]
            xv = w_real * real - w_imag * imag
            xs[half, q] = xv
        out = [copy(f"x_y{i}_{half}", xs.at[half, q], ry.at[half, i], (q, r, c)) for i, q in enumerate(poles)]
        start(*out)
        for q in range(4):
            lanes = slice(q * 128, q * 128 + 128)
            real, imag = acc[half, 0, :, lanes], acc[half, 1, :, lanes]
            xh_, xl_ = split(w_real * real - w_imag * imag)
            yh_, yl_ = split(w_real * imag + w_imag * real)
            xy[q, half * HALF : half * HALF + HALF] = jnp.concatenate([xh_, yh_, xl_, yl_], axis=1)
        return out

    def seat_wait(s):
        pltpu.make_async_remote_copy(
            src_ref=mr.at[s], dst_ref=mr.at[s], send_sem=mssem.at[s], recv_sem=mrsem.at[s],
            device_id=mate, device_id_type=MESH,
        ).wait_recv()

    def seat_pass(s, part, target):
        return pltpu.make_async_remote_copy(
            src_ref=mr.at[s, part], dst_ref=mr.at[s, part], send_sem=mssem.at[s], recv_sem=mrsem.at[s],
            device_id=(p, r, target * 2 + k), device_id_type=MESH,
        )

    steps = [lax.rem(2 * k + s // 2 - h + 4, 4) for s in range(4)]

    def pass_rows():
        for s in range(4):

            @pl.when(steps[s] == 3)
            def _():
                seat_wait(s)
                seat_pass(s, 0, hp).start()

            @pl.when(steps[s] == 1)
            def _():
                seat_wait(s)
                seat_pass(s, 1, hm).start()

    first(0)
    handed(0, ((0, r),))
    start_rows()
    for part in range(2):
        copy(f"g_{part}", graw.at[1 - k, part], graw.at[1 - k, part], mate).wait_recv()
        relayout(1 - k, part)
    first(1)
    early(0)
    second(0)
    early(1)
    second(1)
    middle(0)
    third(0)
    for read in small[3:]:
        read.wait()
    pass_rows()
    late(0)
    x_y = [weigh(0)]
    middle(1)
    third(1)
    late(1)
    x_y.append(weigh(1))

    for s in range(4):

        @pl.when((steps[s] == 2) | ((steps[s] == 0) & (s % 2 != k)))
        def _():
            seat_wait(s)

    bacc[...] = jnp.zeros_like(bacc)

    @pl.loop(0, 4)
    def _(b):
        real, imag = mr[b, 0], mr[b, 1]
        left = jnp.concatenate([real, -imag, real, -imag], axis=1)
        bacc[...] += nt(left, xy[b])

    w_real, w_imag = pw[0, 0], pw[0, 1]
    high, low = split(bacc[...])
    tall = nn(pmat[...], high) + nn(pmat[...], low)
    lead = jnp.where((r == 0) & (c == 0), 1.0, 0.0)
    for node_ in range(4):
        band = slice(node_ * 128, node_ * 128 + 128)
        high, low = split(tall[band])
        chosen = pmat[band]
        own_term = w_real * dg[0, band].astype(F32) - w_imag * dg[1, band].astype(F32)
        term = nt(high, chosen) + nt(low, chosen) + lead * own_term
        dbuf[node_ // 2, (node_ % 2) * 4 : (node_ % 2) * 4 + 4] = term.reshape(4, 4, 8, 128)

    d_core = copy("d_core", dbuf.at[1 - k], dr0, mate)
    start(d_core)
    d_core.wait_recv()
    d1[...] = dbuf[k] + dr0[...]
    d_r = [copy(f"d_r{i}", d1.at[rr], drow.at[i], row(rr)) for i, rr in enumerate(rows)]
    start(*d_r)

    for arrived in d_r:
        arrived.wait_recv()
    d2[...] = d1[r] + ((drow[0] + drow[1]) + (drow[2] + drow[3])) + ((drow[4] + drow[5]) + drow[6])
    for arrived in x_y[0]:
        arrived.wait_recv()
    seat_d = p * 4 + h
    ds[seat_d] = d2[p]
    d_s = [
        copy(f"d_s{i}", d2.at[q], ds.at[seat_d], (q, r, hh * 2 + k))
        for i, (q, hh) in enumerate([(q, hh) for q in [p] + poles for hh in [h] + spans][1:])
    ]
    start(*d_s)

    for arrived in x_y[1]:
        arrived.wait_recv()
    halves = [-((xs[half, p] + ry[half, 0]) + (ry[half, 1] + ry[half, 2])) for half in range(2)]
    high, low = split(jnp.concatenate(halves, axis=0))
    xu[...] = (nn(pmat[...], high) + nn(pmat[...], low)).reshape(4, 2, 64, 128)
    x_z = []
    for turn, which in enumerate((1 - k, k)):
        x_z.append(
            [
                copy(f"x_z{i}_{turn}", xu.at[hh, which], rz.at[turn, i], (p, r, hh * 2 + k))
                for i, hh in enumerate(spans)
            ]
        )
    start(*x_z[0], *x_z[1])

    for arrived in d_s:
        arrived.wait_recv()
    sums = [ds[i] for i in range(16)]
    while len(sums) > 1:
        sums = [sums[i] + sums[i + 1] for i in range(0, len(sums), 2)]
    dfin[k, r, p] = sums[0]
    piece = dfin.at[k, r, p]
    d_p = [copy(f"d_p{i}", piece, piece, (q, r, c)) for i, q in enumerate(poles)]
    start(*d_p)

    spot = k * 4 + p
    for arrived in x_z[0]:
        arrived.wait_recv()
    xz[0] = (xu[h, 1 - k] + rz[0, 0]) + (rz[0, 1] + rz[0, 2])
    x_a = [copy(f"x_a{i}", xz.at[0], outb.at[spot], (q, r, partner)) for i, q in enumerate([p] + poles)]
    start(*x_a)

    for arrived in d_p:
        arrived.wait_recv()
    d_a = [copy(f"d_a{i}", dfin.at[k, r], dfin.at[k, r], row(rr)) for i, rr in enumerate(rows)]
    start(*d_a)

    for arrived in x_z[1]:
        arrived.wait_recv()
    xz[1] = (xu[h, k] + rz[1, 0]) + (rz[1, 1] + rz[1, 2])
    outb[spot] = xz[1]
    x_b = [copy(f"x_b{i}", xz.at[1], outb.at[spot], (q, r, c)) for i, q in enumerate(poles)]
    start(*x_b)

    for arrived in d_a:
        arrived.wait_recv()
    d_c = copy("d_c", dfin.at[k], dfin.at[k], mate)
    start(d_c)

    for arrived in x_a + x_b:
        arrived.wait_recv()
    for b in range(8):
        dens[:, b * 128 : b * 128 + 128] = outb[b]
    d_c.wait_recv()
    diag[...] = dfin[...].reshape(512, 128)

    for done in sent:
        done.wait_send()

    @pl.when(side != k)
    def _():
        row_copy("m_k", partner).wait_send()

    for s in range(4):

        @pl.when((steps[s] == 3) | (steps[s] == 1))
        def _():
            seat_pass(s, 0, hp).wait_send()


def per_device(found_inverse, l_panel, block_pattern, sup_widths, diag_inverse, pole_weights):
    vmem = pl.BlockSpec(memory_space=pltpu.VMEM)
    n = len(NAMES)
    V = pltpu.VMEM
    return pl.pallas_call(
        kernel,
        out_shape=(pltpu.VMEM((64, 1024), F32), pltpu.VMEM((512, 128), F32)),
        in_specs=[pl.BlockSpec(memory_space=pltpu.MemorySpace.HBM)] * 6,
        out_specs=(vmem, vmem),
        scratch_shapes=[
            pltpu.SMEM((4,), jnp.int32),
            pltpu.SMEM((1, 4), jnp.int32),
            pltpu.SMEM((1, 2), F32),
            V((2, 128, 512), BF16),
            V((2, 512, 128), BF16),
            V((2, 2, 512, 8, 128), BF16),
            V((8, 512, 512), BF16),
            V((2, PACKED, 128), BF16),
            V((2, 2, 8, 2, HALF, 128), BF16),
            V((4, 2, PACKED, 128), BF16),
            V((512, PACKED), BF16),
            V((2, 2, HALF, 512), F32),
            V((2, 4, HALF, 128), F32),
            V((4, PACKED, 512), BF16),
            V((PACKED, PACKED), F32),
            V((2, 3, HALF, 128), F32),
            V((4, 2, 64, 128), F32),
            V((2, 3, 64, 128), F32),
            V((2, 64, 128), F32),
            V((8, 64, 128), F32),
            V((2, 8, 4, 8, 128), F32),
            V((8, 4, 8, 128), F32),
            V((8, 4, 8, 128), F32),
            V((7, 4, 8, 128), F32),
            V((4, 8, 128), F32),
            V((16, 8, 128), F32),
            V((2, 8, 4, 8, 128), F32),
            pltpu.SemaphoreType.DMA((7,)),
            pltpu.SemaphoreType.DMA((n,)),
            pltpu.SemaphoreType.DMA((n,)),
            pltpu.SemaphoreType.DMA((4,)),
            pltpu.SemaphoreType.DMA((4,)),
        ],
        compiler_params=pltpu.CompilerParams(
            collective_id=0, has_side_effects=True, vmem_limit_bytes=60000000
        ),
    )(
        sup_widths, block_pattern, pole_weights, l_panel[0], diag_inverse[0],
        found_inverse.reshape(2, 1024, 8, 128),
    )


def solution(mesh):
    in_specs = (
        P("pole", None, "row", None, "col", None),
        P("pole", None, ("row", "col"), None),
        P(("row", "col"), None),
        P(),
        P("pole", None, None, None),
        P("pole", None),
    )
    out_specs = (P("col", "row"), P())
    return jax.shard_map(
        per_device, mesh=mesh, in_specs=in_specs, out_specs=out_specs, check_vma=False
    )
```

```python
import functools

import jax
import jax.numpy as jnp
from jax import lax
from jax.experimental import pallas as pl
from jax.experimental.pallas import tpu as pltpu
from jax.sharding import PartitionSpec as P

MESH = pl.DeviceIdType.MESH
PACKED = 320
F32, BF16 = jnp.float32, jnp.bfloat16


def nt(left, right):
    return lax.dot_general(left, right, (((1,), (1,)), ((), ())), preferred_element_type=F32)


def nn(left, right):
    return lax.dot_general(left, right, (((1,), (0,)), ((), ())), preferred_element_type=F32)


def split(value):
    high = value.astype(BF16)
    return high, (value - high.astype(F32)).astype(BF16)


HALF = PACKED // 2
NAMES = [
    f"{name}_{half}"
    for half in range(2)
    for name in (
        ["c_z", "c_xp", "c_xm", "c_zxp", "c_zxm", "c_x2", "c_x2b", "c_zx2", "c_zx2b"]
        + [f"c_k{i}" for i in range(8)]
        + [f"x_y{i}" for i in range(3)]
        + [f"x_z{i}" for i in range(3)]
    )
]
NAMES += ["g_0", "g_1", "m_p", "m_m", "m_k"] + [f"x_a{i}" for i in range(4)] + [f"x_b{i}" for i in range(3)]
NAMES += ["d_core", "d_c"] + [f"d_r{i}" for i in range(7)] + [f"d_y{i}" for i in range(3)]
NAMES += [f"d_z{i}" for i in range(3)] + [f"d_a{i}" for i in range(7)]
INDEX = {name: i for i, name in enumerate(NAMES)}


def kernel(
    sw_hbm, bp_hbm, pw_hbm, lp_hbm, dg_hbm, g_hbm, dens, diag,
    sw, bp, pw, lp, dg, graw, ga, own, mc, mr, pmat, acc, xs, xy, bacc, ry, xu, rz, xz, outb,
    dbuf, dr0, d1, drow, d2, dy, d3, dz, dfin,
    gsem, ssem, rsem, mssem, mrsem,
):
    p, r, c = lax.axis_index("pole"), lax.axis_index("row"), lax.axis_index("col")
    x, zl = lax.rem(r, 4), lax.div(r, 4)
    h, k = lax.div(c, 2), lax.rem(c, 2)
    up, down, far = lax.rem(x + 1, 4), lax.rem(x + 3, 4), lax.rem(x + 2, 4)
    other = (1 - zl) * 4
    here = zl * 4
    rp, rm, r2 = here + up, here + down, here + far
    rz0, rzp, rzm, rz2 = other + x, other + up, other + down, other + far
    hp, hm = lax.rem(h + 1, 4), lax.rem(h + 3, 4)
    partner = h * 2 + 1 - k
    side = lax.div(h, 2)

    rows = []
    for dz_ in range(2):
        for dx in range(4):
            if (dz_, dx) != (0, 0):
                rows.append(lax.rem(zl + dz_, 2) * 4 + lax.rem(x + dx, 4))
    poles = [lax.rem(p + i, 4) for i in range(1, 4)]
    spans = [lax.rem(h + i, 4) for i in range(1, 4)]
    mates = [(p, partner)] + [(q, cc) for q in poles for cc in (c, partner)]

    def copy(name, src, dst, target, arrive=None):
        i = INDEX[name]
        j = INDEX[arrive or name]
        return pltpu.make_async_remote_copy(
            src_ref=src, dst_ref=dst, send_sem=ssem.at[i], recv_sem=rsem.at[j],
            device_id=target, device_id_type=MESH,
        )

    sent = []

    def start(*copies):
        for each in copies:
            each.start()
            sent.append(each)

    small = [
        pltpu.make_async_copy(src, dst, gsem.at[2 + i])
        for i, (src, dst) in enumerate([(sw_hbm, sw), (bp_hbm, bp), (lp_hbm, lp), (pw_hbm, pw), (dg_hbm, dg)])
    ]
    for read in small:
        read.start()
    near = pl.ds(pl.multiple_of(k * 512, 512), 512)
    away = pl.ds(pl.multiple_of((1 - k) * 512, 512), 512)
    reads = [pltpu.make_async_copy(g_hbm.at[i, near], graw.at[k, i], gsem.at[i]) for i in range(2)]
    for read in reads:
        read.start()

    barrier = pltpu.get_barrier_semaphore()
    peers = [(p, rr, c) for rr in (rp, rm, rz0)] + [(p, r, hh * 2 + k) for hh in spans]
    peers += [(q, r, c) for q in poles] + [(p, r, partner)]
    for peer in peers:
        pl.semaphore_signal(barrier, inc=1, device_id=peer, device_id_type=MESH)

    for read in small[:2]:
        read.wait()
    widths = [sw[i] for i in range(4)]
    starts = [0 * widths[0], widths[0], widths[0] + widths[1], widths[0] + widths[1] + widths[2]]

    def pick(values, which):
        out = jnp.where(which == 0, values[0], values[1])
        out = jnp.where(which == 2, values[2], out)
        return jnp.where(which == 3, values[3], out)

    slot = lax.broadcasted_iota(jnp.int32, (1, 512), 1)
    node, inner = slot // 128, slot % 128
    kept = (inner < pick(widths, node)) & (pick([bp[0, i] for i in range(4)], node) == 1)
    place = jnp.where(kept, pick(starts, node) + inner, -1)
    line = lax.broadcasted_iota(jnp.int32, (PACKED, 512), 0)
    chooser = jnp.where(line == place, 1.0, 0.0).astype(BF16)
    seat = lax.rem(h, 2) * 2 + k
    small[2].wait()
    for part in range(2):
        packed = nt(chooser, lp[part]).astype(BF16)
        own[part] = packed
        for half in range(2):
            mc[half, k, r, part] = packed[half * HALF : half * HALF + HALF]

    @pl.when(side == k)
    def _():
        mr[seat] = own[...]

    pl.semaphore_wait(barrier, len(peers))

    def row(rr):
        return (p, rr, c)

    mate = (p, r, partner)
    for half in range(2):
        mine = mc.at[half, k, r]
        start(
            copy(f"c_z_{half}", mine, mine, row(rz0)),
            copy(f"c_xp_{half}", mine, mine, row(rp)),
            copy(f"c_xm_{half}", mine, mine, row(rm)),
            copy(f"c_k0_{half}", mine, mine, mate),
        )
    start(*[copy(f"g_{i}", g_hbm.at[i, away], graw.at[k, i], mate) for i in range(2)])

    def row_copy(i, target):
        return pltpu.make_async_remote_copy(
            src_ref=own, dst_ref=mr.at[seat], send_sem=ssem.at[INDEX[i]], recv_sem=mrsem.at[seat],
            device_id=(p, r, target), device_id_type=MESH,
        )

    def start_rows():
        start(row_copy("m_p", hp * 2 + side), row_copy("m_m", hm * 2 + side))

        @pl.when(side != k)
        def _():
            row_copy("m_k", partner).start()

    srow = lax.broadcasted_iota(jnp.int32, (512, 1), 0)
    rnode, rinner = srow // 128, srow % 128
    rplace = jnp.where(rinner < pick(widths, rnode), pick(starts, rnode) + rinner, -1)
    across = lax.broadcasted_iota(jnp.int32, (512, PACKED), 1)
    pmat[...] = jnp.where(across == rplace, 1.0, 0.0).astype(BF16)
    acc[...] = jnp.zeros_like(acc)

    def relayout(core, part):
        at = pl.multiple_of((core * 2 + part) * 128, 128)

        @pl.loop(0, 16)
        def _(i):
            band = pl.ds(pl.multiple_of(i * 32, 32), 32)
            block = graw[core, part, band]
            ga[:, band, pl.ds(at, 128)] = jnp.swapaxes(block.astype(F32), 0, 1).astype(BF16)

    for part in range(2):
        reads[part].wait()
        relayout(k, part)

    def arrive(name, half, block):
        ref = mc.at[half, k, block]
        copy(f"{name}_{half}", ref, ref, mate).wait_recv()

    def hand(i, half, block):
        ref = mc.at[half, k, block]
        start(copy(f"c_k{i}_{half}", ref, ref, mate))

    def first(half):
        arrive("c_xp", half, rm)
        ref = mc.at[half, k, rm, 0]
        start(copy(f"c_x2_{half}", ref, ref, row(rp)))
        arrive("c_xm", half, rp)
        ref = mc.at[half, k, rp, 1]
        start(copy(f"c_x2b_{half}", ref, ref, row(rm), f"c_x2_{half}"))
        arrive("c_z", half, rz0)
        ref = mc.at[half, k, rz0]
        start(copy(f"c_zxp_{half}", ref, ref, row(rp)), copy(f"c_zxm_{half}", ref, ref, row(rm)))
        for i, block in ((1, rm), (2, rp), (3, rz0)):
            hand(i, half, block)

    def second(half):
        arrive("c_zxp", half, rzm)
        ref = mc.at[half, k, rzm, 0]
        start(copy(f"c_zx2_{half}", ref, ref, row(rp)))
        arrive("c_zxm", half, rzp)
        ref = mc.at[half, k, rzp, 1]
        start(copy(f"c_zx2b_{half}", ref, ref, row(rm), f"c_zx2_{half}"))
        arrive("c_x2", half, r2)
        for i, block in ((4, rzm), (5, rzp), (6, r2)):
            hand(i, half, block)

    def third(half):
        arrive("c_zx2", half, rz2)
        hand(7, half, rz2)

    def handed(half, which):
        for i, block in which:
            ref = mc.at[half, 1 - k, block]
            copy(f"c_k{i}_{half}", ref, ref, mate).wait_recv()

    def multiply(half, a):
        r0, i0, r1, i1 = mc[half, 0, a, 0], mc[half, 0, a, 1], mc[half, 1, a, 0], mc[half, 1, a, 1]
        right = ga[a]
        acc[half, 0] += nt(jnp.concatenate([r0, -i0, r1, -i1], axis=1), right)
        acc[half, 1] += nt(jnp.concatenate([i0, r0, i1, r1], axis=1), right)

    def early(half):
        handed(half, ((0, r), (1, rm), (2, rp), (3, rz0))[1 - half :])

        @pl.loop(0, 4)
        def _(i):
            multiply(half, jnp.where(i == 0, r, jnp.where(i == 1, rm, jnp.where(i == 2, rp, rz0))))

    def middle(half):
        handed(half, ((4, rzm), (5, rzp), (6, r2)))

        @pl.loop(0, 3)
        def _(i):
            multiply(half, jnp.where(i == 0, rzm, jnp.where(i == 1, rzp, r2)))

    def late(half):
        handed(half, ((7, rz2),))
        multiply(half, rz2)

    def weigh(half):
        w_real, w_imag = pw[0, 0], pw[0, 1]
        for q in range(4):
            lanes = slice(q * 128, q * 128 + 128)
            real, imag = acc[half, 0, :, lanes], acc[half, 1, :, lanes]
            xv = w_real * real - w_imag * imag
            xs[half, q] = xv
        out = [copy(f"x_y{i}_{half}", xs.at[half, q], ry.at[half, i], (q, r, c)) for i, q in enumerate(poles)]
        start(*out)
        for q in range(4):
            lanes = slice(q * 128, q * 128 + 128)
            real, imag = acc[half, 0, :, lanes], acc[half, 1, :, lanes]
            xh_, xl_ = split(w_real * real - w_imag * imag)
            yh_, yl_ = split(w_real * imag + w_imag * real)
            xy[q, half * HALF : half * HALF + HALF] = jnp.concatenate([xh_, yh_, xl_, yl_], axis=1)
        return out

    def seat_wait(s):
        pltpu.make_async_remote_copy(
            src_ref=mr.at[s], dst_ref=mr.at[s], send_sem=mssem.at[s], recv_sem=mrsem.at[s],
            device_id=mate, device_id_type=MESH,
        ).wait_recv()

    def seat_pass(s, part, target):
        return pltpu.make_async_remote_copy(
            src_ref=mr.at[s, part], dst_ref=mr.at[s, part], send_sem=mssem.at[s], recv_sem=mrsem.at[s],
            device_id=(p, r, target * 2 + k), device_id_type=MESH,
        )

    steps = [lax.rem(2 * k + s // 2 - h + 4, 4) for s in range(4)]

    def pass_rows():
        for s in range(4):

            @pl.when(steps[s] == 3)
            def _():
                seat_wait(s)
                seat_pass(s, 0, hp).start()

            @pl.when(steps[s] == 1)
            def _():
                seat_wait(s)
                seat_pass(s, 1, hm).start()

    first(0)
    handed(0, ((0, r),))
    start_rows()
    for part in range(2):
        copy(f"g_{part}", graw.at[1 - k, part], graw.at[1 - k, part], mate).wait_recv()
        relayout(1 - k, part)
    first(1)
    early(0)
    second(0)
    early(1)
    second(1)
    middle(0)
    third(0)
    for read in small[3:]:
        read.wait()
    pass_rows()
    late(0)
    x_y = [weigh(0)]
    middle(1)
    third(1)
    late(1)
    x_y.append(weigh(1))

    for s in range(4):

        @pl.when((steps[s] == 2) | ((steps[s] == 0) & (s % 2 != k)))
        def _():
            seat_wait(s)

    bacc[...] = jnp.zeros_like(bacc)

    @pl.loop(0, 4)
    def _(b):
        real, imag = mr[b, 0], mr[b, 1]
        left = jnp.concatenate([real, -imag, real, -imag], axis=1)
        bacc[...] += nt(left, xy[b])

    w_real, w_imag = pw[0, 0], pw[0, 1]
    high, low = split(bacc[...])
    tall = nn(pmat[...], high) + nn(pmat[...], low)
    lead = jnp.where((r == 0) & (c == 0), 1.0, 0.0)
    for node_ in range(4):
        band = slice(node_ * 128, node_ * 128 + 128)
        high, low = split(tall[band])
        chosen = pmat[band]
        own_term = w_real * dg[0, band].astype(F32) - w_imag * dg[1, band].astype(F32)
        term = nt(high, chosen) + nt(low, chosen) + lead * own_term
        dbuf[node_ // 2, (node_ % 2) * 4 : (node_ % 2) * 4 + 4] = term.reshape(4, 4, 8, 128)

    d_core = copy("d_core", dbuf.at[1 - k], dr0, mate)
    start(d_core)
    d_core.wait_recv()
    d1[...] = dbuf[k] + dr0[...]
    d_r = [copy(f"d_r{i}", d1.at[rr], drow.at[i], row(rr)) for i, rr in enumerate(rows)]
    start(*d_r)

    for arrived in d_r:
        arrived.wait_recv()
    d2[...] = d1[r] + ((drow[0] + drow[1]) + (drow[2] + drow[3])) + ((drow[4] + drow[5]) + drow[6])
    dy[p] = d2[...]
    d_y = [copy(f"d_y{i}", d2, dy.at[p], (q, r, c)) for i, q in enumerate(poles)]
    start(*d_y)

    for arrived in x_y[0]:
        arrived.wait_recv()
    for arrived in x_y[1]:
        arrived.wait_recv()
    halves = [-((xs[half, p] + ry[half, 0]) + (ry[half, 1] + ry[half, 2])) for half in range(2)]
    high, low = split(jnp.concatenate(halves, axis=0))
    xu[...] = (nn(pmat[...], high) + nn(pmat[...], low)).reshape(4, 2, 64, 128)
    x_z = []
    for turn, which in enumerate((1 - k, k)):
        x_z.append(
            [
                copy(f"x_z{i}_{turn}", xu.at[hh, which], rz.at[turn, i], (p, r, hh * 2 + k))
                for i, hh in enumerate(spans)
            ]
        )
    start(*x_z[0], *x_z[1])
    for arrived in d_y:
        arrived.wait_recv()
    d3[...] = (dy[0] + dy[1]) + (dy[2] + dy[3])
    dz[h] = d3[...]
    d_z = [copy(f"d_z{i}", d3, dz.at[h], (p, r, hh * 2 + k)) for i, hh in enumerate(spans)]
    start(*d_z)

    spot = k * 4 + p
    for arrived in x_z[0]:
        arrived.wait_recv()
    xz[0] = (xu[h, 1 - k] + rz[0, 0]) + (rz[0, 1] + rz[0, 2])
    x_a = [copy(f"x_a{i}", xz.at[0], outb.at[spot], (q, r, partner)) for i, q in enumerate([p] + poles)]
    start(*x_a)

    for arrived in x_z[1]:
        arrived.wait_recv()
    xz[1] = (xu[h, k] + rz[1, 0]) + (rz[1, 1] + rz[1, 2])
    outb[spot] = xz[1]
    x_b = [copy(f"x_b{i}", xz.at[1], outb.at[spot], (q, r, c)) for i, q in enumerate(poles)]
    start(*x_b)

    for arrived in d_z:
        arrived.wait_recv()
    dfin[k, r] = (dz[0] + dz[1]) + (dz[2] + dz[3])
    d_a = [copy(f"d_a{i}", dfin.at[k, r], dfin.at[k, r], row(rr)) for i, rr in enumerate(rows)]
    start(*d_a)

    for arrived in x_a + x_b:
        arrived.wait_recv()
    for b in range(8):
        dens[:, b * 128 : b * 128 + 128] = outb[b]

    for arrived in d_a:
        arrived.wait_recv()
    d_c = copy("d_c", dfin.at[k], dfin.at[k], mate)
    start(d_c)
    d_c.wait_recv()
    diag[...] = dfin[...].reshape(512, 128)

    for done in sent:
        done.wait_send()

    @pl.when(side != k)
    def _():
        row_copy("m_k", partner).wait_send()

    for s in range(4):

        @pl.when((steps[s] == 3) | (steps[s] == 1))
        def _():
            seat_pass(s, 0, hp).wait_send()


def per_device(found_inverse, l_panel, block_pattern, sup_widths, diag_inverse, pole_weights):
    vmem = pl.BlockSpec(memory_space=pltpu.VMEM)
    n = len(NAMES)
    V = pltpu.VMEM
    return pl.pallas_call(
        kernel,
        out_shape=(pltpu.VMEM((64, 1024), F32), pltpu.VMEM((512, 128), F32)),
        in_specs=[pl.BlockSpec(memory_space=pltpu.MemorySpace.HBM)] * 6,
        out_specs=(vmem, vmem),
        scratch_shapes=[
            pltpu.SMEM((4,), jnp.int32),
            pltpu.SMEM((1, 4), jnp.int32),
            pltpu.SMEM((1, 2), F32),
            V((2, 128, 512), BF16),
            V((2, 512, 128), BF16),
            V((2, 2, 512, 8, 128), BF16),
            V((8, 512, 512), BF16),
            V((2, PACKED, 128), BF16),
            V((2, 2, 8, 2, HALF, 128), BF16),
            V((4, 2, PACKED, 128), BF16),
            V((512, PACKED), BF16),
            V((2, 2, HALF, 512), F32),
            V((2, 4, HALF, 128), F32),
            V((4, PACKED, 512), BF16),
            V((PACKED, PACKED), F32),
            V((2, 3, HALF, 128), F32),
            V((4, 2, 64, 128), F32),
            V((2, 3, 64, 128), F32),
            V((2, 64, 128), F32),
            V((8, 64, 128), F32),
            V((2, 8, 4, 8, 128), F32),
            V((8, 4, 8, 128), F32),
            V((8, 4, 8, 128), F32),
            V((7, 4, 8, 128), F32),
            V((4, 8, 128), F32),
            V((4, 4, 8, 128), F32),
            V((4, 8, 128), F32),
            V((4, 4, 8, 128), F32),
            V((2, 8, 4, 8, 128), F32),
            pltpu.SemaphoreType.DMA((7,)),
            pltpu.SemaphoreType.DMA((n,)),
            pltpu.SemaphoreType.DMA((n,)),
            pltpu.SemaphoreType.DMA((4,)),
            pltpu.SemaphoreType.DMA((4,)),
        ],
        compiler_params=pltpu.CompilerParams(
            collective_id=0, has_side_effects=True, vmem_limit_bytes=60000000
        ),
    )(
        sup_widths, block_pattern, pole_weights, l_panel[0], diag_inverse[0],
        found_inverse.reshape(2, 1024, 8, 128),
    )


def solution(mesh):
    in_specs = (
        P("pole", None, "row", None, "col", None),
        P("pole", None, ("row", "col"), None),
        P(("row", "col"), None),
        P(),
        P("pole", None, None, None),
        P("pole", None),
    )
    out_specs = (P("col", "row"), P())
    return jax.shard_map(
        per_device, mesh=mesh, in_specs=in_specs, out_specs=out_specs, check_vma=False
    )
```

```python
import functools

import jax
import jax.numpy as jnp
from jax import lax
from jax.experimental import pallas as pl
from jax.experimental.pallas import tpu as pltpu
from jax.sharding import PartitionSpec as P

MESH = pl.DeviceIdType.MESH
PACKED = 320
F32, BF16 = jnp.float32, jnp.bfloat16


def nt(left, right):
    return lax.dot_general(left, right, (((1,), (1,)), ((), ())), preferred_element_type=F32)


def nn(left, right):
    return lax.dot_general(left, right, (((1,), (0,)), ((), ())), preferred_element_type=F32)


def split(value):
    high = value.astype(BF16)
    return high, (value - high.astype(F32)).astype(BF16)


HALF = PACKED // 2
NAMES = [
    f"{name}_{half}"
    for half in range(2)
    for name in (
        ["c_z", "c_xp", "c_xm", "c_zxp", "c_zxm", "c_x2", "c_x2b", "c_zx2", "c_zx2b"]
        + [f"c_k{i}" for i in range(8)]
        + [f"x_y{i}" for i in range(3)]
        + [f"x_z{i}" for i in range(3)]
    )
]
NAMES += ["c_zx2c", "c_zx2d", "g_0", "g_1", "m_p0", "m_p1", "m_m0", "m_m1", "m_k"] + [f"x_a{i}" for i in range(4)] + [f"x_b{i}" for i in range(3)]
NAMES += ["d_core", "d_c"] + [f"d_r{i}" for i in range(7)] + [f"d_y{i}" for i in range(3)]
NAMES += [f"d_z{i}" for i in range(3)] + [f"d_a{i}" for i in range(7)]
INDEX = {name: i for i, name in enumerate(NAMES)}


def kernel(
    sw_hbm, bp_hbm, pw_hbm, lp_hbm, dg_hbm, g_hbm, dens, diag,
    sw, bp, pw, lp, dg, graw, ga, own, mc, mr, pmat, acc, xs, xy, bacc, dterm, ry, xu, rz, xz, outb,
    dbuf, dr0, d1, drow, d2, dy, d3, dz, dfin,
    gsem, ssem, rsem, mssem, mrsem, mrest,
):
    p, r, c = lax.axis_index("pole"), lax.axis_index("row"), lax.axis_index("col")
    x, zl = lax.rem(r, 4), lax.div(r, 4)
    h, k = lax.div(c, 2), lax.rem(c, 2)
    up, down, far = lax.rem(x + 1, 4), lax.rem(x + 3, 4), lax.rem(x + 2, 4)
    other = (1 - zl) * 4
    here = zl * 4
    rp, rm, r2 = here + up, here + down, here + far
    rz0, rzp, rzm, rz2 = other + x, other + up, other + down, other + far
    hp, hm = lax.rem(h + 1, 4), lax.rem(h + 3, 4)
    partner = h * 2 + 1 - k
    side = lax.div(h, 2)

    rows = []
    for dz_ in range(2):
        for dx in range(4):
            if (dz_, dx) != (0, 0):
                rows.append(lax.rem(zl + dz_, 2) * 4 + lax.rem(x + dx, 4))
    poles = [lax.rem(p + i, 4) for i in range(1, 4)]
    spans = [lax.rem(h + i, 4) for i in range(1, 4)]
    mates = [(p, partner)] + [(q, cc) for q in poles for cc in (c, partner)]

    def copy(name, src, dst, target, arrive=None):
        i = INDEX[name]
        j = INDEX[arrive or name]
        return pltpu.make_async_remote_copy(
            src_ref=src, dst_ref=dst, send_sem=ssem.at[i], recv_sem=rsem.at[j],
            device_id=target, device_id_type=MESH,
        )

    sent = []

    def start(*copies):
        for each in copies:
            each.start()
            sent.append(each)

    small = [
        pltpu.make_async_copy(src, dst, gsem.at[2 + i])
        for i, (src, dst) in enumerate([(sw_hbm, sw), (bp_hbm, bp), (lp_hbm, lp), (pw_hbm, pw), (dg_hbm, dg)])
    ]
    for read in small:
        read.start()
    near = pl.ds(pl.multiple_of(k * 512, 512), 512)
    away = pl.ds(pl.multiple_of((1 - k) * 512, 512), 512)
    reads = [pltpu.make_async_copy(g_hbm.at[i, near], graw.at[k, i], gsem.at[i]) for i in range(2)]
    for read in reads:
        read.start()

    barrier = pltpu.get_barrier_semaphore()
    peers = [(p, rr, c) for rr in (rp, rm, rz0)] + [(p, r, hh * 2 + k) for hh in spans]
    peers += [(q, r, c) for q in poles] + [(p, r, partner)]
    for peer in peers:
        pl.semaphore_signal(barrier, inc=1, device_id=peer, device_id_type=MESH)

    for read in small[:2]:
        read.wait()
    widths = [sw[i] for i in range(4)]
    starts = [0 * widths[0], widths[0], widths[0] + widths[1], widths[0] + widths[1] + widths[2]]

    def pick(values, which):
        out = jnp.where(which == 0, values[0], values[1])
        out = jnp.where(which == 2, values[2], out)
        return jnp.where(which == 3, values[3], out)

    slot = lax.broadcasted_iota(jnp.int32, (1, 512), 1)
    node, inner = slot // 128, slot % 128
    kept = (inner < pick(widths, node)) & (pick([bp[0, i] for i in range(4)], node) == 1)
    place = jnp.where(kept, pick(starts, node) + inner, -1)
    line = lax.broadcasted_iota(jnp.int32, (PACKED, 512), 0)
    chooser = jnp.where(line == place, 1.0, 0.0).astype(BF16)
    seat = lax.rem(h, 2) * 2 + k
    small[2].wait()
    for part in range(2):
        packed = nt(chooser, lp[part]).astype(BF16)
        own[part] = packed
        for half in range(2):
            mc[half, k, r, part] = packed[half * HALF : half * HALF + HALF]

    @pl.when(side == k)
    def _():
        mr[seat] = own[...]

    pl.semaphore_wait(barrier, len(peers))

    def row(rr):
        return (p, rr, c)

    mate = (p, r, partner)
    for half in range(2):
        mine = mc.at[half, k, r]
        start(
            copy(f"c_z_{half}", mine, mine, row(rz0)),
            copy(f"c_xp_{half}", mine, mine, row(rp)),
            copy(f"c_xm_{half}", mine, mine, row(rm)),
            copy(f"c_k0_{half}", mine, mine, mate),
        )
    start(*[copy(f"g_{i}", g_hbm.at[i, away], graw.at[k, i], mate) for i in range(2)])

    def row_half(name, part, sem, target):
        return pltpu.make_async_remote_copy(
            src_ref=own.at[part], dst_ref=mr.at[seat, part], send_sem=ssem.at[INDEX[name]], recv_sem=sem.at[seat],
            device_id=(p, r, target), device_id_type=MESH,
        )

    def row_copy(name, target):
        return pltpu.make_async_remote_copy(
            src_ref=own, dst_ref=mr.at[seat], send_sem=ssem.at[INDEX[name]], recv_sem=mrsem.at[seat],
            device_id=(p, r, target), device_id_type=MESH,
        )

    def start_rows():
        start(
            row_half("m_p0", 0, mrsem, hp * 2 + side),
            row_half("m_m1", 1, mrsem, hm * 2 + side),
            row_half("m_p1", 1, mrest, hp * 2 + side),
            row_half("m_m0", 0, mrest, hm * 2 + side),
        )

        @pl.when(side != k)
        def _():
            row_copy("m_k", partner).start()

    srow = lax.broadcasted_iota(jnp.int32, (512, 1), 0)
    rnode, rinner = srow // 128, srow % 128
    rplace = jnp.where(rinner < pick(widths, rnode), pick(starts, rnode) + rinner, -1)
    across = lax.broadcasted_iota(jnp.int32, (512, PACKED), 1)
    pmat[...] = jnp.where(across == rplace, 1.0, 0.0).astype(BF16)
    acc[...] = jnp.zeros_like(acc)

    def relayout(core, part):
        at = pl.multiple_of((core * 2 + part) * 128, 128)

        @pl.loop(0, 16)
        def _(i):
            band = pl.ds(pl.multiple_of(i * 32, 32), 32)
            block = graw[core, part, band]
            ga[:, band, pl.ds(at, 128)] = jnp.swapaxes(block.astype(F32), 0, 1).astype(BF16)

    for part in range(2):
        reads[part].wait()
        relayout(k, part)

    def arrive(name, half, block):
        ref = mc.at[half, k, block]
        copy(f"{name}_{half}", ref, ref, mate).wait_recv()

    def hand(i, half, block):
        ref = mc.at[half, k, block]
        start(copy(f"c_k{i}_{half}", ref, ref, mate))

    def first(half):
        arrive("c_z", half, rz0)
        ref = mc.at[half, k, rz0]
        start(copy(f"c_zxp_{half}", ref, ref, row(rp)), copy(f"c_zxm_{half}", ref, ref, row(rm)))
        arrive("c_xp", half, rm)
        ref = mc.at[half, k, rm, 0]
        start(copy(f"c_x2_{half}", ref, ref, row(rp)))
        arrive("c_xm", half, rp)
        ref = mc.at[half, k, rp, 1]
        start(copy(f"c_x2b_{half}", ref, ref, row(rm), f"c_x2_{half}"))
        for i, block in ((1, rm), (2, rp), (3, rz0)):
            hand(i, half, block)

    def second(half):
        arrive("c_zxp", half, rzm)
        ref = mc.at[half, k, rzm, 0]
        start(copy(f"c_zx2_{half}", ref, ref, row(rp)))
        if half == 1:
            start(copy("c_zx2c", ref, ref, (p, rp, partner), "c_k7_1"))
        arrive("c_zxm", half, rzp)
        ref = mc.at[half, k, rzp, 1]
        start(copy(f"c_zx2b_{half}", ref, ref, row(rm), f"c_zx2_{half}"))
        if half == 1:
            start(copy("c_zx2d", ref, ref, (p, rm, partner), "c_k7_1"))
        arrive("c_x2", half, r2)
        for i, block in ((4, rzm), (5, rzp), (6, r2)):
            hand(i, half, block)

    def third(half):
        arrive("c_zx2", half, rz2)
        if half == 0:
            hand(7, half, rz2)

    def handed(half, which):
        for i, block in which:
            ref = mc.at[half, 1 - k, block]
            copy(f"c_k{i}_{half}", ref, ref, mate).wait_recv()

    def multiply(half, a):
        r0, i0, r1, i1 = mc[half, 0, a, 0], mc[half, 0, a, 1], mc[half, 1, a, 0], mc[half, 1, a, 1]
        right = ga[a]
        acc[half, 0] += nt(jnp.concatenate([r0, -i0, r1, -i1], axis=1), right)
        acc[half, 1] += nt(jnp.concatenate([i0, r0, i1, r1], axis=1), right)

    def early(half):
        handed(half, ((0, r), (1, rm), (2, rp), (3, rz0))[1 - half :])

        @pl.loop(0, 4)
        def _(i):
            multiply(half, jnp.where(i == 0, r, jnp.where(i == 1, rm, jnp.where(i == 2, rp, rz0))))

    def middle(half):
        handed(half, ((4, rzm), (5, rzp), (6, r2)))

        @pl.loop(0, 3)
        def _(i):
            multiply(half, jnp.where(i == 0, rzm, jnp.where(i == 1, rzp, r2)))

    def late(half):
        handed(half, ((7, rz2),))
        multiply(half, rz2)

    def weigh(half):
        w_real, w_imag = pw[0, 0], pw[0, 1]
        for q in range(4):
            lanes = slice(q * 128, q * 128 + 128)
            real, imag = acc[half, 0, :, lanes], acc[half, 1, :, lanes]
            xv = w_real * real - w_imag * imag
            xs[half, q] = xv
        out = [copy(f"x_y{i}_{half}", xs.at[half, q], ry.at[half, i], (q, r, c)) for i, q in enumerate(poles)]
        start(*out)
        for q in range(4):
            lanes = slice(q * 128, q * 128 + 128)
            real, imag = acc[half, 0, :, lanes], acc[half, 1, :, lanes]
            xh_, xl_ = split(w_real * real - w_imag * imag)
            yh_, yl_ = split(w_real * imag + w_imag * real)
            xy[q, half * HALF : half * HALF + HALF] = jnp.concatenate([xh_, yh_, xl_, yl_], axis=1)
        return out

    def seat_wait(s):
        pltpu.make_async_remote_copy(
            src_ref=mr.at[s], dst_ref=mr.at[s], send_sem=mssem.at[s], recv_sem=mrsem.at[s],
            device_id=mate, device_id_type=MESH,
        ).wait_recv()

    def half_wait(s, part, sem):
        pltpu.make_async_remote_copy(
            src_ref=mr.at[s, part], dst_ref=mr.at[s, part], send_sem=mssem.at[s], recv_sem=sem.at[s],
            device_id=mate, device_id_type=MESH,
        ).wait_recv()

    def seat_pass(s, part, target):
        return pltpu.make_async_remote_copy(
            src_ref=mr.at[s, part], dst_ref=mr.at[s, part], send_sem=mssem.at[s], recv_sem=mrsem.at[s],
            device_id=(p, r, target * 2 + k), device_id_type=MESH,
        )

    steps = [lax.rem(2 * k + s // 2 - h + 4, 4) for s in range(4)]

    def pass_rows():
        for s in range(4):

            @pl.when(steps[s] == 3)
            def _():
                half_wait(s, 0, mrsem)
                seat_pass(s, 0, hp).start()

            @pl.when(steps[s] == 1)
            def _():
                half_wait(s, 1, mrsem)
                seat_pass(s, 1, hm).start()

    first(0)
    handed(0, ((0, r),))
    start_rows()
    for part in range(2):
        copy(f"g_{part}", graw.at[1 - k, part], graw.at[1 - k, part], mate).wait_recv()
        relayout(1 - k, part)
    first(1)
    early(0)
    second(0)
    early(1)
    second(1)
    pass_rows()
    middle(0)
    third(0)
    for read in small[3:]:
        read.wait()
    lead = jnp.where((r == 0) & (c == 0), 1.0, 0.0)
    dterm[...] = (lead * pw[0, 0]) * dg[0].astype(F32) - (lead * pw[0, 1]) * dg[1].astype(F32)
    bacc[...] = jnp.zeros_like(bacc)
    late(0)
    x_y = [weigh(0)]
    middle(1)
    third(1)
    late(1)
    x_y.append(weigh(1))

    for s in range(4):

        @pl.when((steps[s] == 2) | ((steps[s] == 0) & (s % 2 != k)))
        def _():
            seat_wait(s)

        @pl.when(steps[s] == 3)
        def _():
            half_wait(s, 1, mrest)

        @pl.when(steps[s] == 1)
        def _():
            half_wait(s, 0, mrest)

    @pl.loop(0, 4)
    def _(b):
        real, imag = mr[b, 0], mr[b, 1]
        left = jnp.concatenate([real, -imag, real, -imag], axis=1)
        bacc[...] += nt(left, xy[b])

    high, low = split(bacc[...])
    tall = nn(pmat[...], high) + nn(pmat[...], low)
    for node_ in range(4):
        band = slice(node_ * 128, node_ * 128 + 128)
        high, low = split(tall[band])
        chosen = pmat[band]
        term = nt(high, chosen) + nt(low, chosen) + dterm[band]
        dbuf[node_ // 2, (node_ % 2) * 4 : (node_ % 2) * 4 + 4] = term.reshape(4, 4, 8, 128)

    d_core = copy("d_core", dbuf.at[1 - k], dr0, mate)
    start(d_core)
    d_core.wait_recv()
    d1[...] = dbuf[k] + dr0[...]
    d_r = [copy(f"d_r{i}", d1.at[rr], drow.at[i], row(rr)) for i, rr in enumerate(rows)]
    start(*d_r)

    for arrived in d_r:
        arrived.wait_recv()
    d2[...] = d1[r] + ((drow[0] + drow[1]) + (drow[2] + drow[3])) + ((drow[4] + drow[5]) + drow[6])
    dy[p] = d2[...]
    d_y = [copy(f"d_y{i}", d2, dy.at[p], (q, r, c)) for i, q in enumerate(poles)]
    start(*d_y)

    for arrived in x_y[0]:
        arrived.wait_recv()
    for arrived in x_y[1]:
        arrived.wait_recv()
    halves = [-((xs[half, p] + ry[half, 0]) + (ry[half, 1] + ry[half, 2])) for half in range(2)]
    high, low = split(jnp.concatenate(halves, axis=0))
    xu[...] = (nn(pmat[...], high) + nn(pmat[...], low)).reshape(4, 2, 64, 128)
    x_z = []
    for turn, which in enumerate((1 - k, k)):
        x_z.append(
            [
                copy(f"x_z{i}_{turn}", xu.at[hh, which], rz.at[turn, i], (p, r, hh * 2 + k))
                for i, hh in enumerate(spans)
            ]
        )
    start(*x_z[0], *x_z[1])
    for arrived in d_y:
        arrived.wait_recv()
    d3[...] = (dy[0] + dy[1]) + (dy[2] + dy[3])
    dz[h] = d3[...]
    d_z = [copy(f"d_z{i}", d3, dz.at[h], (p, r, hh * 2 + k)) for i, hh in enumerate(spans)]
    start(*d_z)

    spot = k * 4 + p
    for arrived in x_z[0]:
        arrived.wait_recv()
    xz[0] = (xu[h, 1 - k] + rz[0, 0]) + (rz[0, 1] + rz[0, 2])
    x_a = [copy(f"x_a{i}", xz.at[0], outb.at[spot], (q, r, partner)) for i, q in enumerate([p] + poles)]
    start(*x_a)

    for arrived in x_z[1]:
        arrived.wait_recv()
    xz[1] = (xu[h, k] + rz[1, 0]) + (rz[1, 1] + rz[1, 2])
    outb[spot] = xz[1]
    x_b = [copy(f"x_b{i}", xz.at[1], outb.at[spot], (q, r, c)) for i, q in enumerate(poles)]
    start(*x_b)

    for arrived in d_z:
        arrived.wait_recv()
    dfin[k, r] = (dz[0] + dz[1]) + (dz[2] + dz[3])
    d_a = [copy(f"d_a{i}", dfin.at[k, r], dfin.at[k, r], row(rr)) for i, rr in enumerate(rows)]
    start(*d_a)

    for arrived in x_a + x_b:
        arrived.wait_recv()
    for b in range(8):
        dens[:, b * 128 : b * 128 + 128] = outb[b]

    for arrived in d_a:
        arrived.wait_recv()
    d_c = copy("d_c", dfin.at[k], dfin.at[k], mate)
    start(d_c)
    d_c.wait_recv()
    diag[...] = dfin[...].reshape(512, 128)

    for done in sent:
        done.wait_send()

    @pl.when(side != k)
    def _():
        row_copy("m_k", partner).wait_send()

    for s in range(4):

        @pl.when((steps[s] == 3) | (steps[s] == 1))
        def _():
            seat_pass(s, 0, hp).wait_send()


def per_device(found_inverse, l_panel, block_pattern, sup_widths, diag_inverse, pole_weights):
    vmem = pl.BlockSpec(memory_space=pltpu.VMEM)
    n = len(NAMES)
    V = pltpu.VMEM
    return pl.pallas_call(
        kernel,
        out_shape=(pltpu.VMEM((64, 1024), F32), pltpu.VMEM((512, 128), F32)),
        in_specs=[pl.BlockSpec(memory_space=pltpu.MemorySpace.HBM)] * 6,
        out_specs=(vmem, vmem),
        scratch_shapes=[
            pltpu.SMEM((4,), jnp.int32),
            pltpu.SMEM((1, 4), jnp.int32),
            pltpu.SMEM((1, 2), F32),
            V((2, 128, 512), BF16),
            V((2, 512, 128), BF16),
            V((2, 2, 512, 8, 128), BF16),
            V((8, 512, 512), BF16),
            V((2, PACKED, 128), BF16),
            V((2, 2, 8, 2, HALF, 128), BF16),
            V((4, 2, PACKED, 128), BF16),
            V((512, PACKED), BF16),
            V((2, 2, HALF, 512), F32),
            V((2, 4, HALF, 128), F32),
            V((4, PACKED, 512), BF16),
            V((PACKED, PACKED), F32),
            V((512, 128), F32),
            V((2, 3, HALF, 128), F32),
            V((4, 2, 64, 128), F32),
            V((2, 3, 64, 128), F32),
            V((2, 64, 128), F32),
            V((8, 64, 128), F32),
            V((2, 8, 4, 8, 128), F32),
            V((8, 4, 8, 128), F32),
            V((8, 4, 8, 128), F32),
            V((7, 4, 8, 128), F32),
            V((4, 8, 128), F32),
            V((4, 4, 8, 128), F32),
            V((4, 8, 128), F32),
            V((4, 4, 8, 128), F32),
            V((2, 8, 4, 8, 128), F32),
            pltpu.SemaphoreType.DMA((7,)),
            pltpu.SemaphoreType.DMA((n,)),
            pltpu.SemaphoreType.DMA((n,)),
            pltpu.SemaphoreType.DMA((4,)),
            pltpu.SemaphoreType.DMA((4,)),
            pltpu.SemaphoreType.DMA((4,)),
        ],
        compiler_params=pltpu.CompilerParams(
            collective_id=0, has_side_effects=True, vmem_limit_bytes=60000000
        ),
    )(
        sup_widths, block_pattern, pole_weights, l_panel[0], diag_inverse[0],
        found_inverse.reshape(2, 1024, 8, 128),
    )


def solution(mesh):
    in_specs = (
        P("pole", None, "row", None, "col", None),
        P("pole", None, ("row", "col"), None),
        P(("row", "col"), None),
        P(),
        P("pole", None, None, None),
        P("pole", None),
    )
    out_specs = (P("col", "row"), P())
    return jax.shard_map(
        per_device, mesh=mesh, in_specs=in_specs, out_specs=out_specs, check_vma=False
    )
```

```python
import functools

import jax
import jax.numpy as jnp
from jax import lax
from jax.experimental import pallas as pl
from jax.experimental.pallas import tpu as pltpu
from jax.sharding import PartitionSpec as P

MESH = pl.DeviceIdType.MESH
PACKED = 320
F32, BF16 = jnp.float32, jnp.bfloat16


def nt(left, right):
    return lax.dot_general(left, right, (((1,), (1,)), ((), ())), preferred_element_type=F32)


def nn(left, right):
    return lax.dot_general(left, right, (((1,), (0,)), ((), ())), preferred_element_type=F32)


def split(value):
    high = value.astype(BF16)
    return high, (value - high.astype(F32)).astype(BF16)


HALF = PACKED // 2
NAMES = [
    f"{name}_{half}"
    for half in range(2)
    for name in (
        ["c_z", "c_xp", "c_xm", "c_zxp", "c_zxm", "c_x2", "c_x2b", "c_zx2", "c_zx2b"]
        + [f"c_k{i}" for i in range(8)]
        + [f"x_y{i}" for i in range(3)]
        + [f"x_z{i}" for i in range(3)]
    )
]
NAMES += ["c_zx2c", "c_zx2d", "g_0", "g_1", "m_p0", "m_p1", "m_m0", "m_m1", "m_k"] + [f"x_a{i}" for i in range(4)] + [f"x_b{i}" for i in range(3)]
NAMES += ["d_core", "d_c"] + [f"d_r{i}" for i in range(7)] + [f"d_y{i}" for i in range(3)]
NAMES += [f"d_z{i}" for i in range(3)] + [f"d_a{i}" for i in range(7)] + [f"d_b{i}" for i in range(7)]
INDEX = {name: i for i, name in enumerate(NAMES)}


def kernel(
    sw_hbm, bp_hbm, pw_hbm, lp_hbm, dg_hbm, g_hbm, dens, diag,
    sw, bp, pw, lp, dg, graw, ga, own, mc, mr, pmat, acc, xs, xy, bacc, dterm, ry, xu, rz, xz, outb,
    dbuf, dr0, d1, drow, d2, dy, d3, dz, dfin,
    gsem, ssem, rsem, mssem, mrsem, mrest,
):
    p, r, c = lax.axis_index("pole"), lax.axis_index("row"), lax.axis_index("col")
    x, zl = lax.rem(r, 4), lax.div(r, 4)
    h, k = lax.div(c, 2), lax.rem(c, 2)
    up, down, far = lax.rem(x + 1, 4), lax.rem(x + 3, 4), lax.rem(x + 2, 4)
    other = (1 - zl) * 4
    here = zl * 4
    rp, rm, r2 = here + up, here + down, here + far
    rz0, rzp, rzm, rz2 = other + x, other + up, other + down, other + far
    hp, hm = lax.rem(h + 1, 4), lax.rem(h + 3, 4)
    partner = h * 2 + 1 - k
    side = lax.div(h, 2)

    rows = []
    for dz_ in range(2):
        for dx in range(4):
            if (dz_, dx) != (0, 0):
                rows.append(lax.rem(zl + dz_, 2) * 4 + lax.rem(x + dx, 4))
    poles = [lax.rem(p + i, 4) for i in range(1, 4)]
    spans = [lax.rem(h + i, 4) for i in range(1, 4)]
    mates = [(p, partner)] + [(q, cc) for q in poles for cc in (c, partner)]

    def copy(name, src, dst, target, arrive=None):
        i = INDEX[name]
        j = INDEX[arrive or name]
        return pltpu.make_async_remote_copy(
            src_ref=src, dst_ref=dst, send_sem=ssem.at[i], recv_sem=rsem.at[j],
            device_id=target, device_id_type=MESH,
        )

    sent = []

    def start(*copies):
        for each in copies:
            each.start()
            sent.append(each)

    small = [
        pltpu.make_async_copy(src, dst, gsem.at[2 + i])
        for i, (src, dst) in enumerate([(sw_hbm, sw), (bp_hbm, bp), (lp_hbm, lp), (pw_hbm, pw), (dg_hbm, dg)])
    ]
    for read in small:
        read.start()
    near = pl.ds(pl.multiple_of(k * 512, 512), 512)
    away = pl.ds(pl.multiple_of((1 - k) * 512, 512), 512)
    reads = [pltpu.make_async_copy(g_hbm.at[i, near], graw.at[k, i], gsem.at[i]) for i in range(2)]
    for read in reads:
        read.start()

    barrier = pltpu.get_barrier_semaphore()
    peers = [(p, rr, c) for rr in (rp, rm, rz0)] + [(p, r, hh * 2 + k) for hh in spans]
    peers += [(q, r, c) for q in poles] + [(p, r, partner)]
    for peer in peers:
        pl.semaphore_signal(barrier, inc=1, device_id=peer, device_id_type=MESH)

    for read in small[:2]:
        read.wait()
    widths = [sw[i] for i in range(4)]
    starts = [0 * widths[0], widths[0], widths[0] + widths[1], widths[0] + widths[1] + widths[2]]

    def pick(values, which):
        out = jnp.where(which == 0, values[0], values[1])
        out = jnp.where(which == 2, values[2], out)
        return jnp.where(which == 3, values[3], out)

    slot = lax.broadcasted_iota(jnp.int32, (1, 512), 1)
    node, inner = slot // 128, slot % 128
    kept = (inner < pick(widths, node)) & (pick([bp[0, i] for i in range(4)], node) == 1)
    place = jnp.where(kept, pick(starts, node) + inner, -1)
    line = lax.broadcasted_iota(jnp.int32, (PACKED, 512), 0)
    chooser = jnp.where(line == place, 1.0, 0.0).astype(BF16)
    seat = lax.rem(h, 2) * 2 + k
    small[2].wait()
    for part in range(2):
        packed = nt(chooser, lp[part]).astype(BF16)
        own[part] = packed
        for half in range(2):
            mc[half, k, r, part] = packed[half * HALF : half * HALF + HALF]

    @pl.when(side == k)
    def _():
        mr[seat] = own[...]

    pl.semaphore_wait(barrier, len(peers))

    def row(rr):
        return (p, rr, c)

    mate = (p, r, partner)
    for half in range(2):
        mine = mc.at[half, k, r]
        start(
            copy(f"c_z_{half}", mine, mine, row(rz0)),
            copy(f"c_xp_{half}", mine, mine, row(rp)),
            copy(f"c_xm_{half}", mine, mine, row(rm)),
            copy(f"c_k0_{half}", mine, mine, mate),
        )
    start(*[copy(f"g_{i}", g_hbm.at[i, away], graw.at[k, i], mate) for i in range(2)])

    def row_half(name, part, sem, target):
        return pltpu.make_async_remote_copy(
            src_ref=own.at[part], dst_ref=mr.at[seat, part], send_sem=ssem.at[INDEX[name]], recv_sem=sem.at[seat],
            device_id=(p, r, target), device_id_type=MESH,
        )

    def row_copy(name, target):
        return pltpu.make_async_remote_copy(
            src_ref=own, dst_ref=mr.at[seat], send_sem=ssem.at[INDEX[name]], recv_sem=mrsem.at[seat],
            device_id=(p, r, target), device_id_type=MESH,
        )

    def start_rows():
        start(
            row_half("m_p0", 0, mrsem, hp * 2 + side),
            row_half("m_m1", 1, mrsem, hm * 2 + side),
            row_half("m_p1", 1, mrest, hp * 2 + side),
            row_half("m_m0", 0, mrest, hm * 2 + side),
        )

        @pl.when(side != k)
        def _():
            row_copy("m_k", partner).start()

    srow = lax.broadcasted_iota(jnp.int32, (512, 1), 0)
    rnode, rinner = srow // 128, srow % 128
    rplace = jnp.where(rinner < pick(widths, rnode), pick(starts, rnode) + rinner, -1)
    across = lax.broadcasted_iota(jnp.int32, (512, PACKED), 1)
    pmat[...] = jnp.where(across == rplace, 1.0, 0.0).astype(BF16)
    acc[...] = jnp.zeros_like(acc)

    def relayout(core, part):
        at = pl.multiple_of((core * 2 + part) * 128, 128)

        @pl.loop(0, 16)
        def _(i):
            band = pl.ds(pl.multiple_of(i * 32, 32), 32)
            block = graw[core, part, band]
            ga[:, band, pl.ds(at, 128)] = jnp.swapaxes(block.astype(F32), 0, 1).astype(BF16)

    for part in range(2):
        reads[part].wait()
        relayout(k, part)

    def arrive(name, half, block):
        ref = mc.at[half, k, block]
        copy(f"{name}_{half}", ref, ref, mate).wait_recv()

    def hand(i, half, block):
        ref = mc.at[half, k, block]
        start(copy(f"c_k{i}_{half}", ref, ref, mate))

    def first(half):
        arrive("c_z", half, rz0)
        ref = mc.at[half, k, rz0]
        start(copy(f"c_zxp_{half}", ref, ref, row(rp)), copy(f"c_zxm_{half}", ref, ref, row(rm)))
        arrive("c_xp", half, rm)
        ref = mc.at[half, k, rm, 0]
        start(copy(f"c_x2_{half}", ref, ref, row(rp)))
        arrive("c_xm", half, rp)
        ref = mc.at[half, k, rp, 1]
        start(copy(f"c_x2b_{half}", ref, ref, row(rm), f"c_x2_{half}"))
        for i, block in ((1, rm), (2, rp), (3, rz0)):
            hand(i, half, block)

    def second(half):
        arrive("c_zxp", half, rzm)
        ref = mc.at[half, k, rzm, 0]
        start(copy(f"c_zx2_{half}", ref, ref, row(rp)))
        if half == 1:
            start(copy("c_zx2c", ref, ref, (p, rp, partner), "c_k7_1"))
        arrive("c_zxm", half, rzp)
        ref = mc.at[half, k, rzp, 1]
        start(copy(f"c_zx2b_{half}", ref, ref, row(rm), f"c_zx2_{half}"))
        if half == 1:
            start(copy("c_zx2d", ref, ref, (p, rm, partner), "c_k7_1"))
        arrive("c_x2", half, r2)
        for i, block in ((4, rzm), (5, rzp), (6, r2)):
            hand(i, half, block)

    def third(half):
        arrive("c_zx2", half, rz2)
        if half == 0:
            hand(7, half, rz2)

    def handed(half, which):
        for i, block in which:
            ref = mc.at[half, 1 - k, block]
            copy(f"c_k{i}_{half}", ref, ref, mate).wait_recv()

    def multiply(half, a):
        r0, i0, r1, i1 = mc[half, 0, a, 0], mc[half, 0, a, 1], mc[half, 1, a, 0], mc[half, 1, a, 1]
        right = ga[a]
        acc[half, 0] += nt(jnp.concatenate([r0, -i0, r1, -i1], axis=1), right)
        acc[half, 1] += nt(jnp.concatenate([i0, r0, i1, r1], axis=1), right)

    def early(half):
        handed(half, ((0, r), (1, rm), (2, rp), (3, rz0))[1 - half :])

        @pl.loop(0, 4)
        def _(i):
            multiply(half, jnp.where(i == 0, r, jnp.where(i == 1, rm, jnp.where(i == 2, rp, rz0))))

    def middle(half):
        handed(half, ((4, rzm), (5, rzp), (6, r2)))

        @pl.loop(0, 3)
        def _(i):
            multiply(half, jnp.where(i == 0, rzm, jnp.where(i == 1, rzp, r2)))

    def late(half):
        handed(half, ((7, rz2),))
        multiply(half, rz2)

    def weigh(half):
        w_real, w_imag = pw[0, 0], pw[0, 1]
        for q in range(4):
            lanes = slice(q * 128, q * 128 + 128)
            real, imag = acc[half, 0, :, lanes], acc[half, 1, :, lanes]
            xv = w_real * real - w_imag * imag
            xs[half, q] = xv
        out = [copy(f"x_y{i}_{half}", xs.at[half, q], ry.at[half, i], (q, r, c)) for i, q in enumerate(poles)]
        start(*out)
        for q in range(4):
            lanes = slice(q * 128, q * 128 + 128)
            real, imag = acc[half, 0, :, lanes], acc[half, 1, :, lanes]
            xh_, xl_ = split(w_real * real - w_imag * imag)
            yh_, yl_ = split(w_real * imag + w_imag * real)
            xy[q, half * HALF : half * HALF + HALF] = jnp.concatenate([xh_, yh_, xl_, yl_], axis=1)
        return out

    def seat_wait(s):
        pltpu.make_async_remote_copy(
            src_ref=mr.at[s], dst_ref=mr.at[s], send_sem=mssem.at[s], recv_sem=mrsem.at[s],
            device_id=mate, device_id_type=MESH,
        ).wait_recv()

    def half_wait(s, part, sem):
        pltpu.make_async_remote_copy(
            src_ref=mr.at[s, part], dst_ref=mr.at[s, part], send_sem=mssem.at[s], recv_sem=sem.at[s],
            device_id=mate, device_id_type=MESH,
        ).wait_recv()

    def seat_pass(s, part, target):
        return pltpu.make_async_remote_copy(
            src_ref=mr.at[s, part], dst_ref=mr.at[s, part], send_sem=mssem.at[s], recv_sem=mrsem.at[s],
            device_id=(p, r, target * 2 + k), device_id_type=MESH,
        )

    steps = [lax.rem(2 * k + s // 2 - h + 4, 4) for s in range(4)]

    def pass_rows():
        for s in range(4):

            @pl.when(steps[s] == 3)
            def _():
                half_wait(s, 0, mrsem)
                seat_pass(s, 0, hp).start()

            @pl.when(steps[s] == 1)
            def _():
                half_wait(s, 1, mrsem)
                seat_pass(s, 1, hm).start()

    first(0)
    handed(0, ((0, r),))
    start_rows()
    for part in range(2):
        copy(f"g_{part}", graw.at[1 - k, part], graw.at[1 - k, part], mate).wait_recv()
        relayout(1 - k, part)
    first(1)
    early(0)
    second(0)
    early(1)
    second(1)
    pass_rows()
    middle(0)
    third(0)
    for read in small[3:]:
        read.wait()
    lead = jnp.where((r == 0) & (c == 0), 1.0, 0.0)
    dterm[...] = (lead * pw[0, 0]) * dg[0].astype(F32) - (lead * pw[0, 1]) * dg[1].astype(F32)
    bacc[...] = jnp.zeros_like(bacc)
    late(0)
    x_y = [weigh(0)]
    middle(1)
    third(1)
    late(1)
    x_y.append(weigh(1))

    for s in range(4):

        @pl.when((steps[s] == 2) | ((steps[s] == 0) & (s % 2 != k)))
        def _():
            seat_wait(s)

        @pl.when(steps[s] == 3)
        def _():
            half_wait(s, 1, mrest)

        @pl.when(steps[s] == 1)
        def _():
            half_wait(s, 0, mrest)

    @pl.loop(0, 4)
    def _(b):
        real, imag = mr[b, 0], mr[b, 1]
        left = jnp.concatenate([real, -imag, real, -imag], axis=1)
        bacc[...] += nt(left, xy[b])

    high, low = split(bacc[...])
    tall = nn(pmat[...], high) + nn(pmat[...], low)
    for node_ in range(4):
        band = slice(node_ * 128, node_ * 128 + 128)
        high, low = split(tall[band])
        chosen = pmat[band]
        term = nt(high, chosen) + nt(low, chosen) + dterm[band]
        dbuf[node_ // 2, (node_ % 2) * 4 : (node_ % 2) * 4 + 4] = term.reshape(4, 4, 8, 128)

    d_core = copy("d_core", dbuf.at[1 - k], dr0, mate)
    start(d_core)
    d_core.wait_recv()
    d1[...] = dbuf[k] + dr0[...]
    d_r = [copy(f"d_r{i}", d1.at[rr], drow.at[i], row(rr)) for i, rr in enumerate(rows)]
    start(*d_r)

    for arrived in d_r:
        arrived.wait_recv()
    d2[...] = d1[r] + ((drow[0] + drow[1]) + (drow[2] + drow[3])) + ((drow[4] + drow[5]) + drow[6])
    dy[p] = d2[...]
    d_y = [copy(f"d_y{i}", d2, dy.at[p], (q, r, c)) for i, q in enumerate(poles)]
    start(*d_y)

    for arrived in x_y[0]:
        arrived.wait_recv()
    for arrived in x_y[1]:
        arrived.wait_recv()
    halves = [-((xs[half, p] + ry[half, 0]) + (ry[half, 1] + ry[half, 2])) for half in range(2)]
    high, low = split(jnp.concatenate(halves, axis=0))
    xu[...] = (nn(pmat[...], high) + nn(pmat[...], low)).reshape(4, 2, 64, 128)
    x_z = []
    for turn, which in enumerate((1 - k, k)):
        x_z.append(
            [
                copy(f"x_z{i}_{turn}", xu.at[hh, which], rz.at[turn, i], (p, r, hh * 2 + k))
                for i, hh in enumerate(spans)
            ]
        )
    start(*x_z[0], *x_z[1])
    for arrived in d_y:
        arrived.wait_recv()
    d3[...] = (dy[0] + dy[1]) + (dy[2] + dy[3])
    dz[h] = d3[...]
    d_z = [copy(f"d_z{i}", d3, dz.at[h], (p, r, hh * 2 + k)) for i, hh in enumerate(spans)]
    start(*d_z)

    spot = k * 4 + p
    for arrived in x_z[0]:
        arrived.wait_recv()
    xz[0] = (xu[h, 1 - k] + rz[0, 0]) + (rz[0, 1] + rz[0, 2])
    x_a = [copy(f"x_a{i}", xz.at[0], outb.at[spot], (q, r, partner)) for i, q in enumerate([p] + poles)]
    start(*x_a)

    for arrived in x_z[1]:
        arrived.wait_recv()
    xz[1] = (xu[h, k] + rz[1, 0]) + (rz[1, 1] + rz[1, 2])
    outb[spot] = xz[1]
    x_b = [copy(f"x_b{i}", xz.at[1], outb.at[spot], (q, r, c)) for i, q in enumerate(poles)]
    start(*x_b)

    for arrived in d_z:
        arrived.wait_recv()
    dfin[k, r] = (dz[0] + dz[1]) + (dz[2] + dz[3])
    piece = dfin.at[k, r]
    d_a = [copy(f"d_a{i}", piece, piece, row(rr)) for i, rr in enumerate(rows)]
    d_b = [copy(f"d_b{i}", piece, piece, (p, rr, partner)) for i, rr in enumerate(rows)]
    for pair in zip(d_a, d_b):
        start(*pair)
    d_c = copy("d_c", piece, piece, mate)
    start(d_c)

    for arrived in x_a + x_b:
        arrived.wait_recv()
    for b in range(8):
        dens[:, b * 128 : b * 128 + 128] = outb[b]

    for arrived in d_a + d_b + [d_c]:
        arrived.wait_recv()
    diag[...] = dfin[...].reshape(512, 128)

    for done in sent:
        done.wait_send()

    @pl.when(side != k)
    def _():
        row_copy("m_k", partner).wait_send()

    for s in range(4):

        @pl.when((steps[s] == 3) | (steps[s] == 1))
        def _():
            seat_pass(s, 0, hp).wait_send()


def per_device(found_inverse, l_panel, block_pattern, sup_widths, diag_inverse, pole_weights):
    vmem = pl.BlockSpec(memory_space=pltpu.VMEM)
    n = len(NAMES)
    V = pltpu.VMEM
    return pl.pallas_call(
        kernel,
        out_shape=(pltpu.VMEM((64, 1024), F32), pltpu.VMEM((512, 128), F32)),
        in_specs=[pl.BlockSpec(memory_space=pltpu.MemorySpace.HBM)] * 6,
        out_specs=(vmem, vmem),
        scratch_shapes=[
            pltpu.SMEM((4,), jnp.int32),
            pltpu.SMEM((1, 4), jnp.int32),
            pltpu.SMEM((1, 2), F32),
            V((2, 128, 512), BF16),
            V((2, 512, 128), BF16),
            V((2, 2, 512, 8, 128), BF16),
            V((8, 512, 512), BF16),
            V((2, PACKED, 128), BF16),
            V((2, 2, 8, 2, HALF, 128), BF16),
            V((4, 2, PACKED, 128), BF16),
            V((512, PACKED), BF16),
            V((2, 2, HALF, 512), F32),
            V((2, 4, HALF, 128), F32),
            V((4, PACKED, 512), BF16),
            V((PACKED, PACKED), F32),
            V((512, 128), F32),
            V((2, 3, HALF, 128), F32),
            V((4, 2, 64, 128), F32),
            V((2, 3, 64, 128), F32),
            V((2, 64, 128), F32),
            V((8, 64, 128), F32),
            V((2, 8, 4, 8, 128), F32),
            V((8, 4, 8, 128), F32),
            V((8, 4, 8, 128), F32),
            V((7, 4, 8, 128), F32),
            V((4, 8, 128), F32),
            V((4, 4, 8, 128), F32),
            V((4, 8, 128), F32),
            V((4, 4, 8, 128), F32),
            V((2, 8, 4, 8, 128), F32),
            pltpu.SemaphoreType.DMA((7,)),
            pltpu.SemaphoreType.DMA((n,)),
            pltpu.SemaphoreType.DMA((n,)),
            pltpu.SemaphoreType.DMA((4,)),
            pltpu.SemaphoreType.DMA((4,)),
            pltpu.SemaphoreType.DMA((4,)),
        ],
        compiler_params=pltpu.CompilerParams(
            collective_id=0, has_side_effects=True, vmem_limit_bytes=60000000
        ),
    )(
        sup_widths, block_pattern, pole_weights, l_panel[0], diag_inverse[0],
        found_inverse.reshape(2, 1024, 8, 128),
    )


def solution(mesh):
    in_specs = (
        P("pole", None, "row", None, "col", None),
        P("pole", None, ("row", "col"), None),
        P(("row", "col"), None),
        P(),
        P("pole", None, None, None),
        P("pole", None),
    )
    out_specs = (P("col", "row"), P())
    return jax.shard_map(
        per_device, mesh=mesh, in_specs=in_specs, out_specs=out_specs, check_vma=False
    )
```
